512 devices in a mesh: grp: 4 (over x), own: 128 (over z, y, core).
Axes of the slice: x: 4, y: 4, z: 16, core: 2. Of those that a mesh axis runs over, the one named last changes fastest.
Arguments:
- tile_row: int32 [4, 128, 24576], P('grp', 'own'), may hold values from 0 to 7
- pixel_col: int32 [4, 128, 24576], P('grp', 'own'), may hold values from 0 to 16383
- weight: bfloat16 [4, 128, 24576], P('grp', 'own'), may hold values from 0.25 to 4
- counts: int32 [4, 128, 128], P('grp', 'own'), may hold values from 1 to 192
- kernel: float32 [9, 9], replicated, may hold values from 0.01 to 0.05
Outputs:
- smoothed: float32 [1024, 16384], P('own', 'grp')
The draws below stay inside these ranges and needn't reach their ends.
Inputs may be any that keep to these rules, and one draw needn't show every extreme that they name: `counts`: slots past a block's count hold unused values.
All inputs are finite; a program needn't handle non-finite values.
Results may differ from the reference program's by a relative error of at most 0.0012.
Values may be sent and summed in bfloat16 or wider, within the bound.
No kernel may reach another device: no remote copies, remote signals or barrier semaphores. Data moves between devices by JAX's collectives and lax.ppermute only.
A program may use at most 64 MiB of HBM per device.

```python
import math
import jax
import jax.numpy as jnp

W = 16384
STRIP = 8
CAP = 192
NROWS = 1024
N_GRP = 4
N_OWN = 128


def with_ends(array, rng, low, top_value):
    place = [jax.random.randint(jax.random.fold_in(rng, axis), (), 0, length) for axis, length in enumerate(array.shape)]
    longest = array.shape.index(max(array.shape))
    neighbour = place[:longest] + [(place[longest] + 1) % array.shape[longest]] + place[longest + 1:]
    return array.at[tuple(place)].set(low).at[tuple(neighbour)].set(top_value)


def level_of(own_key, shape, shards, least, high):
    level = 1.0
    for dim, parts in shards:
        steps = jax.random.uniform(jax.random.fold_in(jax.random.fold_in(own_key, 6), dim), (parts,), jnp.float32, least / len(shards), high / len(shards))
        level = level * jnp.repeat(jnp.exp(steps), shape[dim] // parts).reshape((-1,) + (1,) * (len(shape) - 1 - dim))
    return level


def setup_inputs(seed: int = 0) -> dict:
    seeds = jax.random.split(jax.random.key(seed), 6)
    return {
        "tile_row": with_ends(jax.random.randint(seeds[0], (N_GRP, N_OWN, N_OWN * CAP), 0, STRIP), jax.random.fold_in(seeds[0], 1), 0, STRIP - 1).astype(jnp.int32),
        "pixel_col": with_ends(jax.random.randint(seeds[1], (N_GRP, N_OWN, N_OWN * CAP), 0, W), jax.random.fold_in(seeds[1], 1), 0, W - 1).astype(jnp.int32),
        "weight": jnp.clip(jnp.exp(math.log(4.0) - 2.7725887 * jax.random.uniform(seeds[2], (N_GRP, N_OWN, N_OWN * CAP), jnp.float32) ** level_of(seeds[2], (N_GRP, N_OWN, N_OWN * CAP), ((0, 4), (1, 128)), -0.2, 0.2)), 0.25, 4.0).astype(jnp.bfloat16),
        "counts": with_ends(jax.random.randint(seeds[3], (N_GRP, N_OWN, N_OWN), 1, CAP + 1), jax.random.fold_in(seeds[3], 1), 1, CAP).astype(jnp.int32),
        "kernel": jnp.clip(jax.random.uniform(seeds[4], (9, 9), jnp.float32, 0.01, 0.05), 0.01, 0.05),
    }


def reference(tile_row, pixel_col, weight, counts, kernel):
    slot_count = tile_row.shape[2]
    slot_ids = jnp.arange(slot_count, dtype=jnp.int32)
    dest_ids = slot_ids // CAP
    live = (slot_ids % CAP)[None, None, :] < jnp.repeat(counts, CAP, axis=2)
    grid_row = dest_ids[None, None, :] * STRIP + tile_row
    flat_index = (grid_row * W + pixel_col).astype(jnp.int32).reshape(-1)
    values = jnp.where(live, weight.astype(jnp.float32), jnp.zeros((), jnp.float32)).reshape(-1)
    heat = jax.ops.segment_sum(values, flat_index, num_segments=NROWS * W).reshape(NROWS, W)
    padded = jnp.pad(heat, 4)
    smoothed = jnp.zeros((NROWS, W), jnp.float32)
    for a in range(9):
        for b in range(9):
            smoothed = smoothed + kernel[a, b] * padded[a:a + NROWS, b:b + W]
    return smoothed
```

```python
import jax
import jax.numpy as jnp
from jax import lax
from jax.experimental import pallas as pl
from jax.experimental.pallas import tpu as pltpu
from jax.sharding import PartitionSpec as P

W = 16384
STRIP = 8
CAP = 192
LANES = 128
HALO = 4
SPAN = 256
CELLS = STRIP * W // SPAN
ROWS = 8


def vmem_spec():
    return pl.BlockSpec(memory_space=pltpu.VMEM)


def smem_spec():
    return pl.BlockSpec(memory_space=pltpu.SMEM)


def pack_kernel(row_ref, col_ref, weight_ref, count_ref, out_ref, wide_ref):
    points = row_ref.shape[0]
    pairs = points // 3
    for i in range(points):
        wide_ref[pl.ds(i, 1), :] = weight_ref[i].astype(jnp.float32)
    lane = lax.broadcasted_iota(jnp.int32, (pairs, LANES), 1)
    block = lax.broadcasted_iota(jnp.int32, (pairs, LANES), 0)
    counts = jnp.broadcast_to(count_ref[...], (pairs, LANES))
    even = jnp.sum(jnp.where(lane == 2 * block, counts, 0), axis=1, keepdims=True)
    odd = jnp.sum(jnp.where(lane == 2 * block + 1, counts, 0), axis=1, keepdims=True)
    low = lane < 64
    lives = (
        lane < even,
        jnp.where(low, lane + 128, lane - 64) < jnp.where(low, even, odd),
        lane + 64 < odd,
    )
    ids, masses = [], []
    for k in range(3):
        tile_row = row_ref[pl.ds(k, pairs, stride=3), :]
        column = col_ref[pl.ds(k, pairs, stride=3), :]
        index = ((column // SPAN) * STRIP + tile_row) * SPAN + column % SPAN
        ids.append(index.astype(jnp.float32))
        masses.append(jnp.where(lives[k], wide_ref[pl.ds(k, pairs, stride=3), :], 0.0))
    half = LANES // 2
    out_ref[pl.ds(0, pairs, stride=6), :] = ids[0]
    out_ref[pl.ds(1, pairs, stride=6), :] = jnp.where(low, ids[1], pltpu.roll(masses[1], half, 1))
    out_ref[pl.ds(2, pairs, stride=6), :] = masses[0]
    out_ref[pl.ds(3, pairs, stride=6), :] = ids[2]
    out_ref[pl.ds(4, pairs, stride=6), :] = jnp.where(low, pltpu.roll(ids[1], half, 1), masses[1])
    out_ref[pl.ds(5, pairs, stride=6), :] = masses[2]


def bin_kernel(points_ref, out_ref, first_ref, second_ref, mass_ref, acc_ref):
    sources = points_ref.shape[0] // 3
    half = sources // 2
    low = lax.broadcasted_iota(jnp.int32, (half, LANES), 1) < 64
    upper = points_ref[pl.ds(1, half, stride=3), :]
    lower = points_ref[pl.ds(1 + 3 * half, half, stride=3), :]
    mixed_ids = jnp.where(low, upper, pltpu.roll(lower, 64, 1))
    mixed_masses = jnp.where(low, pltpu.roll(upper, 64, 1), lower)
    for ids, masses, at in (
        (points_ref[pl.ds(0, sources, stride=3), :], points_ref[pl.ds(2, sources, stride=3), :], 0),
        (mixed_ids, mixed_masses, sources),
    ):
        ids = ids.astype(jnp.int32)
        here = pl.ds(at, ids.shape[0])
        first_ref[here, :] = (ids // SPAN).astype(jnp.float32) - 256.0
        second_ref[here, :] = (ids % SPAN).astype(jnp.float32)
        mass_ref[here, :] = masses
    first_iota = (
        lax.broadcasted_iota(jnp.int32, (CELLS, LANES), 0).astype(jnp.float32) - 256.0
    ).astype(jnp.bfloat16)
    second_iota = lax.broadcasted_iota(jnp.int32, (SPAN, LANES), 0).astype(jnp.float32).astype(jnp.bfloat16)
    one = jnp.ones((), jnp.bfloat16)
    zero = jnp.zeros((), jnp.bfloat16)
    acc_ref[...] = jnp.zeros_like(acc_ref)

    def step(i, carry):
        here = pl.ds(pl.multiple_of(i * ROWS, ROWS), ROWS)
        first = first_ref[here, :].astype(jnp.bfloat16)
        second = second_ref[here, :].astype(jnp.bfloat16)
        mass = mass_ref[here, :].astype(jnp.bfloat16)
        left, right = [], []
        for r in range(ROWS):
            left.append(jnp.where(first_iota == first[r : r + 1], one, zero))
            right.append(jnp.where(second_iota == second[r : r + 1], mass[r : r + 1], zero))
        acc_ref[...] += lax.dot_general(
            jnp.concatenate(left, axis=1),
            jnp.concatenate(right, axis=1),
            (((1,), (1,)), ((), ())),
            preferred_element_type=jnp.float32,
        )
        return carry

    lax.fori_loop(0, first_ref.shape[0] // ROWS, step, 0)
    quarters, _, width = out_ref.shape
    span = width - LANES
    groups = span // SPAN
    low8 = lax.broadcasted_iota(jnp.int32, (STRIP, LANES), 1) < 64
    blank = jnp.zeros((STRIP, LANES), jnp.float32)
    for q in range(quarters):
        for c in range(groups):
            at = (q * groups + c) * STRIP
            out_ref[q, :, c * SPAN : (c + 1) * SPAN] = acc_ref[at : at + STRIP, :].astype(jnp.bfloat16)
        at = q * groups * STRIP
        before = acc_ref[at - STRIP : at, LANES:] if q else blank
        at += groups * STRIP
        after = acc_ref[at : at + STRIP, :LANES] if q < quarters - 1 else blank
        out_ref[q, :, span:] = jnp.where(low8, after, before).astype(jnp.bfloat16)


def sum_kernel(parity_ref, parts_ref, sum_ref, near_ref, far_ref):
    total = parts_ref[0].astype(jnp.float32)
    for g in range(1, parts_ref.shape[0]):
        total = total + parts_ref[g].astype(jnp.float32)
    sum_ref[...] = total
    top = total[:HALO]
    bottom = total[HALO:]
    is_odd = parity_ref[0] == 1
    near_ref[...] = jnp.where(is_odd, top, bottom).astype(jnp.bfloat16)
    far_ref[...] = jnp.where(is_odd, bottom, top).astype(jnp.bfloat16)


def smooth_kernel(parity_ref, kernel_ref, own_ref, near_ref, far_ref, out_ref):
    own = own_ref[...]
    near = near_ref[...].astype(jnp.float32)
    far = far_ref[...].astype(jnp.float32)
    is_odd = parity_ref[0] == 1
    above = jnp.where(is_odd, near, far)
    below = jnp.where(is_odd, far, near)
    frame = jnp.concatenate([above, own, below], axis=0)
    width = frame.shape[1]
    wins = [frame[a : a + STRIP] for a in range(9)]
    total = None
    for b in range(9):
        part = kernel_ref[0, b] * wins[0]
        for a in range(1, 9):
            part = part + kernel_ref[a, b] * wins[a]
        shift = (HALO - b) % width
        part = pltpu.roll(part, shift, 1) if shift else part
        total = part if total is None else total + part
    out_ref[...] = total[:, : out_ref.shape[1]]


def per_device(tile_row, pixel_col, weight, counts, kernel):
    owners = lax.axis_size("own")
    groups = lax.axis_size("grp")
    points = tile_row.shape[2] // LANES
    quarter = W // groups
    width = quarter + LANES
    packed = pl.pallas_call(
        pack_kernel,
        out_shape=jax.ShapeDtypeStruct((3 * owners, LANES), jnp.float32),
        in_specs=[vmem_spec()] * 4,
        out_specs=vmem_spec(),
        scratch_shapes=[pltpu.VMEM((points, LANES), jnp.float32)],
        name="pack",
    )(
        tile_row.reshape(points, LANES),
        pixel_col.reshape(points, LANES),
        weight.reshape(points, 1, LANES),
        counts.reshape(1, owners),
    )
    arrived = lax.all_to_all(
        packed.reshape(3 * owners, 1, LANES), "own", split_axis=0, concat_axis=0, tiled=True
    ).reshape(3 * owners, LANES)
    parts = pl.pallas_call(
        bin_kernel,
        out_shape=jax.ShapeDtypeStruct((groups, STRIP, width), jnp.bfloat16),
        in_specs=[vmem_spec()],
        out_specs=vmem_spec(),
        scratch_shapes=[pltpu.VMEM((points, LANES), jnp.float32)] * 3
        + [pltpu.VMEM((CELLS, SPAN), jnp.float32)],
        compiler_params=pltpu.CompilerParams(vmem_limit_bytes=48 * 2**20),
        name="bin",
    )(arrived)
    parts = lax.all_to_all(parts, "grp", split_axis=0, concat_axis=0, tiled=True)
    me = lax.axis_index("own")
    parity = (me % 2).reshape(1).astype(jnp.int32)
    own, near, far = pl.pallas_call(
        sum_kernel,
        out_shape=(
            jax.ShapeDtypeStruct((STRIP, width), jnp.float32),
            jax.ShapeDtypeStruct((HALO, width), jnp.bfloat16),
            jax.ShapeDtypeStruct((HALO, width), jnp.bfloat16),
        ),
        in_specs=[smem_spec(), vmem_spec()],
        out_specs=(vmem_spec(),) * 3,
        name="total",
    )(parity, parts)
    on_chip = [(i, i ^ 1) for i in range(owners)]
    across = [(i, i + 1) for i in range(1, owners - 1, 2)]
    across = across + [(j, i) for i, j in across]
    near = lax.ppermute(near, "own", on_chip)
    far = lax.ppermute(far, "own", across)
    return pl.pallas_call(
        smooth_kernel,
        out_shape=jax.ShapeDtypeStruct((STRIP, quarter), jnp.float32),
        in_specs=[smem_spec(), smem_spec()] + [vmem_spec()] * 3,
        out_specs=vmem_spec(),
        name="smooth",
    )(parity, kernel, own, near, far)


def solution(mesh):
    placed = (
        P("grp", "own", None),
        P("grp", "own", None),
        P("grp", "own", None),
        P("grp", "own", None),
        P(),
    )
    return jax.shard_map(
        per_device, mesh=mesh, in_specs=placed, out_specs=P("own", "grp"), check_vma=False
    )
```

```python
import jax
import jax.numpy as jnp
from jax import lax
from jax.experimental import pallas as pl
from jax.experimental.pallas import tpu as pltpu
from jax.sharding import PartitionSpec as P

W = 16384
STRIP = 8
CAP = 192
LANES = 128
HALO = 4
TAPS = 2 * HALO + 1
PARTS = 32
TERM = 48
SPAN = 256
CELLS = STRIP * W // SPAN
ROWS = 64


def vmem_spec():
    return pl.BlockSpec(memory_space=pltpu.VMEM)


def smem_spec():
    return pl.BlockSpec(memory_space=pltpu.SMEM)


def limit(mebibytes):
    return pltpu.CompilerParams(vmem_limit_bytes=mebibytes * 2**20)


def pack_kernel(row_ref, col_ref, weight_ref, count_ref, out_ref, wide_ref):
    points = row_ref.shape[0]
    pairs = points // 3
    for i in range(points):
        wide_ref[pl.ds(i, 1), :] = weight_ref[i].astype(jnp.float32)
    lane = lax.broadcasted_iota(jnp.int32, (pairs, LANES), 1)
    block = lax.broadcasted_iota(jnp.int32, (pairs, LANES), 0)
    counts = jnp.broadcast_to(count_ref[...], (pairs, LANES))
    even = jnp.sum(jnp.where(lane == 2 * block, counts, 0), axis=1, keepdims=True)
    odd = jnp.sum(jnp.where(lane == 2 * block + 1, counts, 0), axis=1, keepdims=True)
    low = lane < 64
    lives = (
        lane < even,
        jnp.where(low, lane + 128, lane - 64) < jnp.where(low, even, odd),
        lane + 64 < odd,
    )
    ids, masses = [], []
    for k in range(3):
        tile_row = row_ref[pl.ds(k, pairs, stride=3), :]
        column = col_ref[pl.ds(k, pairs, stride=3), :]
        index = (((column >> 8) * STRIP + tile_row) << 8) + (column & 255)
        ids.append(index.astype(jnp.float32))
        masses.append(jnp.where(lives[k], wide_ref[pl.ds(k, pairs, stride=3), :], 0.0))
    half = LANES // 2
    out_ref[pl.ds(0, pairs, stride=6), :] = ids[0]
    out_ref[pl.ds(1, pairs, stride=6), :] = jnp.where(low, ids[1], pltpu.roll(masses[1], half, 1))
    out_ref[pl.ds(2, pairs, stride=6), :] = masses[0]
    out_ref[pl.ds(3, pairs, stride=6), :] = ids[2]
    out_ref[pl.ds(4, pairs, stride=6), :] = jnp.where(low, pltpu.roll(ids[1], half, 1), masses[1])
    out_ref[pl.ds(5, pairs, stride=6), :] = masses[2]


def bin_kernel(points_ref, out_ref, first_ref, second_ref, mass_ref, acc_ref):
    sources = points_ref.shape[0] // 3
    half = sources // 2
    low = lax.broadcasted_iota(jnp.int32, (half, LANES), 1) < 64
    upper = points_ref[pl.ds(1, half, stride=3), :]
    lower = points_ref[pl.ds(1 + 3 * half, half, stride=3), :]
    mixed_ids = jnp.where(low, upper, pltpu.roll(lower, 64, 1))
    mixed_masses = jnp.where(low, pltpu.roll(upper, 64, 1), lower)
    for ids, masses, at in (
        (points_ref[pl.ds(0, sources, stride=3), :], points_ref[pl.ds(2, sources, stride=3), :], 0),
        (mixed_ids, mixed_masses, sources),
    ):
        ids = ids.astype(jnp.int32)
        here = pl.ds(at, ids.shape[0])
        first_ref[here, :] = ((ids >> 8) - 256).astype(jnp.float32)
        second_ref[here, :] = (ids & 255).astype(jnp.float32)
        mass_ref[here, :] = masses
    first_iota = (
        lax.broadcasted_iota(jnp.int32, (CELLS, LANES), 0).astype(jnp.float32) - 256.0
    ).astype(jnp.bfloat16)
    second_iota = lax.broadcasted_iota(jnp.int32, (SPAN, LANES), 0).astype(jnp.float32).astype(jnp.bfloat16)
    one = jnp.ones((), jnp.bfloat16)
    zero = jnp.zeros((), jnp.bfloat16)
    acc_ref[...] = jnp.zeros_like(acc_ref)

    def step(i, carry):
        here = pl.ds(pl.multiple_of(i * ROWS, ROWS), ROWS)
        first = first_ref[here, :].astype(jnp.bfloat16)
        second = second_ref[here, :].astype(jnp.bfloat16)
        mass = mass_ref[here, :].astype(jnp.bfloat16)
        left, right = [], []
        for r in range(ROWS):
            left.append(jnp.where(first_iota == first[r : r + 1], one, zero))
            right.append(jnp.where(second_iota == second[r : r + 1], mass[r : r + 1], zero))
        acc_ref[...] += lax.dot_general(
            jnp.concatenate(left, axis=1),
            jnp.concatenate(right, axis=1),
            (((1,), (1,)), ((), ())),
            preferred_element_type=jnp.float32,
        )
        return carry

    lax.fori_loop(0, first_ref.shape[0] // ROWS, step, 0)
    width = out_ref.shape[1]
    quarters = out_ref.shape[0] // STRIP
    span = width - LANES
    groups = span // SPAN
    low8 = lax.broadcasted_iota(jnp.int32, (STRIP, LANES), 1) < 64
    blank = jnp.zeros((STRIP, LANES), jnp.float32)
    for q in range(quarters):
        rows = pl.ds(q * STRIP, STRIP)
        for c in range(groups):
            at = (q * groups + c) * STRIP
            out_ref[rows, c * SPAN : (c + 1) * SPAN] = acc_ref[at : at + STRIP, :].astype(jnp.bfloat16)
        at = q * groups * STRIP
        before = acc_ref[at - STRIP : at, LANES:] if q else blank
        at += groups * STRIP
        after = acc_ref[at : at + STRIP, :LANES] if q < quarters - 1 else blank
        out_ref[rows, span:] = jnp.where(low8, after, before).astype(jnp.bfloat16)


def band_kernel(parity_ref, kernel_ref, band_ref, odd_ref):
    parity = parity_ref[0]
    row = lax.broadcasted_iota(jnp.int32, (STRIP, 3 * TERM), 0)
    lane = lax.broadcasted_iota(jnp.int32, (STRIP, 3 * TERM), 1)
    source = lane % TERM
    near = source - PARTS
    far = near - HALO
    near = near + (1 - parity) * (STRIP + HALO)
    far = far + parity * (STRIP + HALO)
    framed = jnp.where(
        source < PARTS,
        HALO + source % STRIP,
        jnp.where(source < PARTS + HALO, near, jnp.where(source < PARTS + 2 * HALO, far, -STRIP)),
    )
    tap = framed - row
    for b in range(TAPS):
        whole = jnp.zeros(tap.shape, jnp.float32)
        for a in range(TAPS):
            whole = jnp.where(tap == a, kernel_ref[a, b], whole)
        high = whole.astype(jnp.bfloat16).astype(jnp.float32)
        rest = whole - high
        middle = rest.astype(jnp.bfloat16).astype(jnp.float32)
        term = jnp.where(lane < TERM, high, jnp.where(lane < 2 * TERM, middle, rest - middle))
        band_ref[pl.ds(b * STRIP, STRIP), :] = term
    odd_ref[...] = jnp.broadcast_to(parity.astype(jnp.float32), odd_ref.shape)


def sum_kernel(odd_ref, parts_ref, near_ref, far_ref):
    is_odd = odd_ref[:HALO, :] > 0.5
    for t in range(parts_ref.shape[1] // LANES):
        here = slice(t * LANES, (t + 1) * LANES)
        total = parts_ref[:STRIP, here].astype(jnp.float32)
        for g in range(1, parts_ref.shape[0] // STRIP):
            total = total + parts_ref[g * STRIP : (g + 1) * STRIP, here].astype(jnp.float32)
        top = total[:HALO]
        bottom = total[HALO:]
        near_ref[:, here] = jnp.where(is_odd, top, bottom).astype(jnp.bfloat16)
        far_ref[:, here] = jnp.where(is_odd, bottom, top).astype(jnp.bfloat16)


def smooth_kernel(band_ref, parts_ref, near_ref, far_ref, out_ref):
    width = parts_ref.shape[1]
    near = near_ref[...].astype(jnp.float32)
    far = far_ref[...].astype(jnp.float32)
    blank = jnp.zeros((STRIP, width), jnp.float32)
    halo = jnp.concatenate([near, far, blank], axis=0).astype(jnp.bfloat16)
    frame = jnp.concatenate([parts_ref[...], halo], axis=0)
    frame = jnp.concatenate([frame, frame, frame], axis=0)
    shifted = jnp.dot(band_ref[...].astype(jnp.bfloat16), frame, preferred_element_type=jnp.float32)
    total = shifted[HALO * STRIP : (HALO + 1) * STRIP]
    for b in range(TAPS):
        if b != HALO:
            part = shifted[b * STRIP : (b + 1) * STRIP]
            total = total + pltpu.roll(part, (HALO - b) % width, 1)
    out_ref[...] = total[:, : out_ref.shape[1]]


def per_device(tile_row, pixel_col, weight, counts, kernel):
    owners = lax.axis_size("own")
    groups = lax.axis_size("grp")
    points = tile_row.shape[2] // LANES
    quarter = W // groups
    width = quarter + LANES
    packed = pl.pallas_call(
        pack_kernel,
        out_shape=jax.ShapeDtypeStruct((3 * owners, LANES), jnp.float32),
        in_specs=[vmem_spec()] * 4,
        out_specs=vmem_spec(),
        scratch_shapes=[pltpu.VMEM((points, LANES), jnp.float32)],
        compiler_params=limit(4),
        name="pack",
    )(
        tile_row.reshape(points, LANES),
        pixel_col.reshape(points, LANES),
        weight.reshape(points, 1, LANES),
        counts.reshape(1, owners),
    )
    arrived = lax.all_to_all(
        packed.reshape(3 * owners, 1, LANES), "own", split_axis=0, concat_axis=0, tiled=True
    ).reshape(3 * owners, LANES)
    parts = pl.pallas_call(
        bin_kernel,
        out_shape=jax.ShapeDtypeStruct((groups * STRIP, width), jnp.bfloat16),
        in_specs=[vmem_spec()],
        out_specs=vmem_spec(),
        scratch_shapes=[pltpu.VMEM((points, LANES), jnp.float32)] * 3
        + [pltpu.VMEM((CELLS, SPAN), jnp.float32)],
        compiler_params=limit(32),
        name="bin",
    )(arrived)
    sent, kernel = lax.optimization_barrier((parts, kernel))
    parts = lax.all_to_all(sent, "grp", split_axis=0, concat_axis=0, tiled=True)
    parity = (lax.axis_index("own") & 1).reshape(1).astype(jnp.int32)
    band, odd = pl.pallas_call(
        band_kernel,
        out_shape=(
            jax.ShapeDtypeStruct((TAPS * STRIP, 3 * TERM), jnp.float32),
            jax.ShapeDtypeStruct((STRIP, LANES), jnp.float32),
        ),
        in_specs=[smem_spec(), smem_spec()],
        out_specs=(vmem_spec(),) * 2,
        compiler_params=limit(4),
        name="band",
    )(parity, kernel)
    near, far = pl.pallas_call(
        sum_kernel,
        out_shape=(jax.ShapeDtypeStruct((HALO, width), jnp.bfloat16),) * 2,
        in_specs=[vmem_spec()] * 2,
        out_specs=(vmem_spec(),) * 2,
        compiler_params=limit(4),
        name="total",
    )(odd, parts)
    on_chip = [(i, i ^ 1) for i in range(owners)]
    across = [(i, i + 1) for i in range(1, owners - 1, 2)]
    across = across + [(j, i) for i, j in across]
    far = lax.ppermute(far, "own", across)
    near = lax.ppermute(near, "own", on_chip)
    return pl.pallas_call(
        smooth_kernel,
        out_shape=jax.ShapeDtypeStruct((STRIP, quarter), jnp.float32),
        in_specs=[vmem_spec()] * 4,
        out_specs=vmem_spec(),
        compiler_params=limit(16),
        name="smooth",
    )(band, parts, near, far)


def solution(mesh):
    placed = (
        P("grp", "own", None),
        P("grp", "own", None),
        P("grp", "own", None),
        P("grp", "own", None),
        P(),
    )
    return jax.shard_map(
        per_device, mesh=mesh, in_specs=placed, out_specs=P("own", "grp"), check_vma=False
    )
```

```python
import functools

import jax
import jax.numpy as jnp
from jax import lax
from jax.experimental import pallas as pl
from jax.experimental.pallas import tpu as pltpu
from jax.sharding import PartitionSpec as P

W = 16384
STRIP = 8
CAP = 192
LANES = 128
HALO = 4
TAPS = 2 * HALO + 1
PARTS = 32
TERM = 48
SPAN = 256
CELLS = STRIP * W // SPAN
ROWS = 96


def vmem_spec():
    return pl.BlockSpec(memory_space=pltpu.VMEM)


def smem_spec():
    return pl.BlockSpec(memory_space=pltpu.SMEM)


def limit(mebibytes):
    return pltpu.CompilerParams(vmem_limit_bytes=mebibytes * 2**20)


def pack_kernel(row_in, col_in, weight_in, count_in, out_ref, row_ref, col_ref, weight_ref, count_ref, wide_ref, sems):
    copies = [
        pltpu.make_async_copy(source, target, sems.at[i])
        for i, (source, target) in enumerate(
            ((weight_in, weight_ref), (count_in, count_ref), (row_in, row_ref), (col_in, col_ref))
        )
    ]
    for copy in copies:
        copy.start()
    for copy in copies:
        copy.wait()
    points = row_ref.shape[0]
    pairs = points // 3
    for i in range(points):
        wide_ref[pl.ds(i, 1), :] = weight_ref[i].astype(jnp.float32)
    lane = lax.broadcasted_iota(jnp.int32, (pairs, LANES), 1)
    block = lax.broadcasted_iota(jnp.int32, (pairs, LANES), 0)
    counts = jnp.broadcast_to(count_ref[...], (pairs, LANES))
    even = jnp.sum(jnp.where(lane == 2 * block, counts, 0), axis=1, keepdims=True)
    odd = jnp.sum(jnp.where(lane == 2 * block + 1, counts, 0), axis=1, keepdims=True)
    low = lane < 64
    lives = (
        lane < even,
        jnp.where(low, lane + 128, lane - 64) < jnp.where(low, even, odd),
        lane + 64 < odd,
    )
    ids, masses = [], []
    for k in range(3):
        tile_row = row_ref[pl.ds(k, pairs, stride=3), :]
        column = col_ref[pl.ds(k, pairs, stride=3), :]
        index = (((column >> 8) * STRIP + tile_row) << 8) + (column & 255)
        ids.append(index.astype(jnp.float32))
        masses.append(jnp.where(lives[k], wide_ref[pl.ds(k, pairs, stride=3), :], 0.0))
    half = LANES // 2
    out_ref[pl.ds(0, pairs, stride=6), :] = ids[0]
    out_ref[pl.ds(1, pairs, stride=6), :] = jnp.where(low, ids[1], pltpu.roll(masses[1], half, 1))
    out_ref[pl.ds(2, pairs, stride=6), :] = masses[0]
    out_ref[pl.ds(3, pairs, stride=6), :] = ids[2]
    out_ref[pl.ds(4, pairs, stride=6), :] = jnp.where(low, pltpu.roll(ids[1], half, 1), masses[1])
    out_ref[pl.ds(5, pairs, stride=6), :] = masses[2]


def bin_kernel(points_ref, out_ref, first_ref, second_ref, mass_ref, acc_ref):
    sources = points_ref.shape[0] // 3
    half = sources // 2
    low = lax.broadcasted_iota(jnp.int32, (half, LANES), 1) < 64
    upper = points_ref[pl.ds(1, half, stride=3), :]
    lower = points_ref[pl.ds(1 + 3 * half, half, stride=3), :]
    mixed_ids = jnp.where(low, upper, pltpu.roll(lower, 64, 1))
    mixed_masses = jnp.where(low, pltpu.roll(upper, 64, 1), lower)
    for ids, masses, at in (
        (points_ref[pl.ds(0, sources, stride=3), :], points_ref[pl.ds(2, sources, stride=3), :], 0),
        (mixed_ids, mixed_masses, sources),
    ):
        ids = ids.astype(jnp.int32)
        here = pl.ds(at, ids.shape[0])
        first_ref[here, :] = ((ids >> 8) - 256).astype(jnp.float32)
        second_ref[here, :] = (ids & 255).astype(jnp.float32)
        mass_ref[here, :] = masses
    first_iota = (
        lax.broadcasted_iota(jnp.int32, (CELLS, LANES), 0).astype(jnp.float32) - 256.0
    ).astype(jnp.bfloat16)
    second_iota = lax.broadcasted_iota(jnp.int32, (SPAN, LANES), 0).astype(jnp.float32).astype(jnp.bfloat16)
    one = jnp.ones((), jnp.bfloat16)
    zero = jnp.zeros((), jnp.bfloat16)
    acc_ref[...] = jnp.zeros_like(acc_ref)

    def step(i, carry):
        here = pl.ds(pl.multiple_of(i * ROWS, ROWS), ROWS)
        first = first_ref[here, :].astype(jnp.bfloat16)
        second = second_ref[here, :].astype(jnp.bfloat16)
        mass = mass_ref[here, :].astype(jnp.bfloat16)
        left, right = [], []
        for r in range(ROWS):
            left.append(jnp.where(first_iota == first[r : r + 1], one, zero))
            right.append(jnp.where(second_iota == second[r : r + 1], mass[r : r + 1], zero))
        acc_ref[...] += lax.dot_general(
            jnp.concatenate(left, axis=1),
            jnp.concatenate(right, axis=1),
            (((1,), (1,)), ((), ())),
            preferred_element_type=jnp.float32,
        )
        return carry

    lax.fori_loop(0, first_ref.shape[0] // ROWS, step, 0)
    width = out_ref.shape[1]
    quarters = out_ref.shape[0] // STRIP
    span = width - LANES
    groups = span // SPAN
    low8 = lax.broadcasted_iota(jnp.int32, (STRIP, LANES), 1) < 64
    blank = jnp.zeros((STRIP, LANES), jnp.float32)
    for q in range(quarters):
        rows = pl.ds(q * STRIP, STRIP)
        for c in range(groups):
            at = (q * groups + c) * STRIP
            out_ref[rows, c * SPAN : (c + 1) * SPAN] = acc_ref[at : at + STRIP, :].astype(jnp.bfloat16)
        at = q * groups * STRIP
        before = acc_ref[at - STRIP : at, LANES:] if q else blank
        at += groups * STRIP
        after = acc_ref[at : at + STRIP, :LANES] if q < quarters - 1 else blank
        out_ref[rows, span:] = jnp.where(low8, after, before).astype(jnp.bfloat16)


def band_kernel(parity_ref, kernel_ref, band_ref, odd_ref):
    parity = parity_ref[0]
    row = lax.broadcasted_iota(jnp.int32, (STRIP, 3 * TERM), 0)
    lane = lax.broadcasted_iota(jnp.int32, (STRIP, 3 * TERM), 1)
    source = lane % TERM
    near = source - PARTS
    far = near - HALO
    near = near + (1 - parity) * (STRIP + HALO)
    far = far + parity * (STRIP + HALO)
    framed = jnp.where(
        source < PARTS,
        HALO + source % STRIP,
        jnp.where(source < PARTS + HALO, near, jnp.where(source < PARTS + 2 * HALO, far, -STRIP)),
    )
    tap = framed - row
    for b in range(TAPS):
        whole = jnp.zeros(tap.shape, jnp.float32)
        for a in range(TAPS):
            whole = jnp.where(tap == a, kernel_ref[a, b], whole)
        high = whole.astype(jnp.bfloat16).astype(jnp.float32)
        rest = whole - high
        middle = rest.astype(jnp.bfloat16).astype(jnp.float32)
        term = jnp.where(lane < TERM, high, jnp.where(lane < 2 * TERM, middle, rest - middle))
        band_ref[pl.ds(b * STRIP, STRIP), :] = term
    odd_ref[...] = jnp.broadcast_to(parity.astype(jnp.float32), odd_ref.shape)


def edge_kernel(odd_ref, parts_ref, edge_ref, *, top_if_odd):
    is_top = (odd_ref[:HALO, :] > 0.5) == top_if_odd
    for t in range(parts_ref.shape[1] // LANES):
        here = slice(t * LANES, (t + 1) * LANES)
        total = parts_ref[:STRIP, here].astype(jnp.float32)
        for g in range(1, parts_ref.shape[0] // STRIP):
            total = total + parts_ref[g * STRIP : (g + 1) * STRIP, here].astype(jnp.float32)
        edge_ref[:, here] = jnp.where(is_top, total[:HALO], total[HALO:]).astype(jnp.bfloat16)


def smooth_kernel(band_ref, parts_ref, near_ref, far_ref, out_ref):
    width = parts_ref.shape[1]
    near = near_ref[...].astype(jnp.float32)
    far = far_ref[...].astype(jnp.float32)
    blank = jnp.zeros((STRIP, width), jnp.float32)
    halo = jnp.concatenate([near, far, blank], axis=0).astype(jnp.bfloat16)
    frame = jnp.concatenate([parts_ref[...], halo], axis=0)
    frame = jnp.concatenate([frame, frame, frame], axis=0)
    shifted = jnp.dot(band_ref[...].astype(jnp.bfloat16), frame, preferred_element_type=jnp.float32)
    total = shifted[HALO * STRIP : (HALO + 1) * STRIP]
    for b in range(TAPS):
        if b != HALO:
            part = shifted[b * STRIP : (b + 1) * STRIP]
            total = total + pltpu.roll(part, (HALO - b) % width, 1)
    out_ref[...] = total[:, : out_ref.shape[1]]


def per_device(tile_row, pixel_col, weight, counts, kernel):
    owners = lax.axis_size("own")
    groups = lax.axis_size("grp")
    points = tile_row.shape[2] // LANES
    quarter = W // groups
    width = quarter + LANES
    packed = pl.pallas_call(
        pack_kernel,
        out_shape=jax.ShapeDtypeStruct((3 * owners, LANES), jnp.float32),
        in_specs=[pl.BlockSpec(memory_space=pltpu.HBM)] * 4,
        out_specs=vmem_spec(),
        scratch_shapes=[
            pltpu.VMEM((points, LANES), jnp.int32),
            pltpu.VMEM((points, LANES), jnp.int32),
            pltpu.VMEM((points, 1, LANES), jnp.bfloat16),
            pltpu.VMEM((1, owners), jnp.int32),
            pltpu.VMEM((points, LANES), jnp.float32),
            pltpu.SemaphoreType.DMA((4,)),
        ],
        compiler_params=limit(4),
        name="pack",
    )(
        *(
            pltpu.with_memory_space_constraint(value.reshape(shape), pltpu.HBM)
            for value, shape in (
                (tile_row, (points, LANES)),
                (pixel_col, (points, LANES)),
                (weight, (points, 1, LANES)),
                (counts, (1, owners)),
            )
        )
    )
    arrived = lax.all_to_all(
        packed.reshape(3 * owners, 1, LANES), "own", split_axis=0, concat_axis=0, tiled=True
    ).reshape(3 * owners, LANES)
    parts = pl.pallas_call(
        bin_kernel,
        out_shape=jax.ShapeDtypeStruct((groups * STRIP, width), jnp.bfloat16),
        in_specs=[vmem_spec()],
        out_specs=vmem_spec(),
        scratch_shapes=[pltpu.VMEM((points, LANES), jnp.float32)] * 3
        + [pltpu.VMEM((CELLS, SPAN), jnp.float32)],
        compiler_params=limit(32),
        name="bin",
    )(arrived)
    sent, kernel = lax.optimization_barrier((parts, kernel))
    parts = lax.all_to_all(sent, "grp", split_axis=0, concat_axis=0, tiled=True)
    parity = (lax.axis_index("own") & 1).reshape(1).astype(jnp.int32)
    band, odd = pl.pallas_call(
        band_kernel,
        out_shape=(
            jax.ShapeDtypeStruct((TAPS * STRIP, 3 * TERM), jnp.float32),
            jax.ShapeDtypeStruct((STRIP, LANES), jnp.float32),
        ),
        in_specs=[smem_spec(), smem_spec()],
        out_specs=(vmem_spec(),) * 2,
        compiler_params=limit(4),
        name="band",
    )(parity, kernel)
    def edge(parts, top_if_odd, name):
        return pl.pallas_call(
            functools.partial(edge_kernel, top_if_odd=top_if_odd),
            out_shape=jax.ShapeDtypeStruct((HALO, width), jnp.bfloat16),
            in_specs=[vmem_spec()] * 2,
            out_specs=vmem_spec(),
            compiler_params=limit(4),
            name=name,
        )(odd, parts)

    near = edge(parts, True, "near")
    near, later = lax.optimization_barrier((near, parts))
    far = edge(later, False, "far")
    on_chip = [(i, i ^ 1) for i in range(owners)]
    across = [(i, i + 1) for i in range(1, owners - 1, 2)]
    across = across + [(j, i) for i, j in across]
    far = lax.ppermute(far, "own", across)
    near = lax.ppermute(near, "own", on_chip)
    return pl.pallas_call(
        smooth_kernel,
        out_shape=jax.ShapeDtypeStruct((STRIP, quarter), jnp.float32),
        in_specs=[vmem_spec()] * 4,
        out_specs=vmem_spec(),
        compiler_params=limit(16),
        name="smooth",
    )(band, parts, near, far)


def solution(mesh):
    placed = (
        P("grp", "own", None),
        P("grp", "own", None),
        P("grp", "own", None),
        P("grp", "own", None),
        P(),
    )
    return jax.shard_map(
        per_device, mesh=mesh, in_specs=placed, out_specs=P("own", "grp"), check_vma=False
    )
```

```python
import functools

import jax
import jax.numpy as jnp
from jax import lax
from jax.experimental import pallas as pl
from jax.experimental.pallas import tpu as pltpu
from jax.sharding import PartitionSpec as P

W = 16384
STRIP = 8
CAP = 192
LANES = 128
HALO = 4
TAPS = 2 * HALO + 1
PARTS = 40
TERM = 48
SPAN = 256
CELLS = STRIP * W // SPAN
ROWS = 96
OWN_ROWS = 96


def vmem_spec():
    return pl.BlockSpec(memory_space=pltpu.VMEM)


def smem_spec():
    return pl.BlockSpec(memory_space=pltpu.SMEM)


def limit(mebibytes):
    return pltpu.CompilerParams(vmem_limit_bytes=mebibytes * 2**20)


def pack_kernel(row_in, col_in, weight_in, count_in, out_ref, row_ref, col_ref, weight_ref, count_ref, wide_ref, sems):
    copies = [
        pltpu.make_async_copy(source, target, sems.at[i])
        for i, (source, target) in enumerate(
            ((weight_in, weight_ref), (count_in, count_ref), (row_in, row_ref), (col_in, col_ref))
        )
    ]
    for copy in copies:
        copy.start()
    for copy in copies:
        copy.wait()
    points = row_ref.shape[0]
    pairs = points // 3
    for i in range(points):
        wide_ref[pl.ds(i, 1), :] = weight_ref[i].astype(jnp.float32)
    lane = lax.broadcasted_iota(jnp.int32, (pairs, LANES), 1)
    block = lax.broadcasted_iota(jnp.int32, (pairs, LANES), 0)
    counts = jnp.broadcast_to(count_ref[...], (pairs, LANES))
    even = jnp.sum(jnp.where(lane == 2 * block, counts, 0), axis=1, keepdims=True)
    odd = jnp.sum(jnp.where(lane == 2 * block + 1, counts, 0), axis=1, keepdims=True)
    low = lane < 64
    lives = (
        lane < even,
        jnp.where(low, lane + 128, lane - 64) < jnp.where(low, even, odd),
        lane + 64 < odd,
    )
    ids, masses = [], []
    for k in range(3):
        tile_row = row_ref[pl.ds(k, pairs, stride=3), :]
        column = col_ref[pl.ds(k, pairs, stride=3), :]
        index = (((column >> 8) * STRIP + tile_row) << 8) + (column & 255)
        ids.append(index.astype(jnp.float32))
        masses.append(jnp.where(lives[k], wide_ref[pl.ds(k, pairs, stride=3), :], 0.0))
    half = LANES // 2
    out_ref[pl.ds(0, pairs, stride=6), :] = ids[0]
    out_ref[pl.ds(1, pairs, stride=6), :] = jnp.where(low, ids[1], pltpu.roll(masses[1], half, 1))
    out_ref[pl.ds(2, pairs, stride=6), :] = masses[0]
    out_ref[pl.ds(3, pairs, stride=6), :] = ids[2]
    out_ref[pl.ds(4, pairs, stride=6), :] = jnp.where(low, pltpu.roll(ids[1], half, 1), masses[1])
    out_ref[pl.ds(5, pairs, stride=6), :] = masses[2]


def one_hot_sum(acc_ref, first_ref, second_ref, mass_ref, rows):
    cells = acc_ref.shape[0]
    first_iota = (
        lax.broadcasted_iota(jnp.int32, (cells, LANES), 0).astype(jnp.float32) - 256.0
    ).astype(jnp.bfloat16)
    second_iota = lax.broadcasted_iota(jnp.int32, (SPAN, LANES), 0).astype(jnp.float32).astype(jnp.bfloat16)
    one = jnp.ones((), jnp.bfloat16)
    zero = jnp.zeros((), jnp.bfloat16)
    acc_ref[...] = jnp.zeros_like(acc_ref)

    def step(i, carry):
        here = pl.ds(pl.multiple_of(i * rows, rows), rows)
        first = first_ref[here, :].astype(jnp.bfloat16)
        second = second_ref[here, :].astype(jnp.bfloat16)
        mass = mass_ref[here, :].astype(jnp.bfloat16)
        left, right = [], []
        for r in range(rows):
            left.append(jnp.where(first_iota == first[r : r + 1], one, zero))
            right.append(jnp.where(second_iota == second[r : r + 1], mass[r : r + 1], zero))
        acc_ref[...] += lax.dot_general(
            jnp.concatenate(left, axis=1),
            jnp.concatenate(right, axis=1),
            (((1,), (1,)), ((), ())),
            preferred_element_type=jnp.float32,
        )
        return carry

    lax.fori_loop(0, first_ref.shape[0] // rows, step, 0)


def store_strip(out_ref, rows, acc_ref, at, before, after):
    span = out_ref.shape[1] - LANES
    for c in range(span // SPAN):
        block = acc_ref[at + c * STRIP : at + (c + 1) * STRIP, :]
        out_ref[rows, c * SPAN : (c + 1) * SPAN] = block.astype(jnp.bfloat16)
    low = lax.broadcasted_iota(jnp.int32, (STRIP, LANES), 1) < 64
    out_ref[rows, span:] = jnp.where(low, after, before).astype(jnp.bfloat16)


def others_kernel(points_ref, out_ref, side_ref, first_ref, second_ref, mass_ref, acc_ref):
    quarters = out_ref.shape[0] // STRIP
    here = lax.axis_index("grp")
    share = CELLS // quarters
    sources = points_ref.shape[0] // 3
    half = sources // 2
    low = lax.broadcasted_iota(jnp.int32, (half, LANES), 1) < 64
    upper = points_ref[pl.ds(1, half, stride=3), :]
    lower = points_ref[pl.ds(1 + 3 * half, half, stride=3), :]
    mixed_ids = jnp.where(low, upper, pltpu.roll(lower, 64, 1))
    mixed_masses = jnp.where(low, pltpu.roll(upper, 64, 1), lower)
    origin = (here + 1) * share - STRIP
    for ids, masses, at in (
        (points_ref[pl.ds(0, sources, stride=3), :], points_ref[pl.ds(2, sources, stride=3), :], 0),
        (mixed_ids, mixed_masses, sources),
    ):
        ids = ids.astype(jnp.int32)
        rows = pl.ds(at, ids.shape[0])
        first = ((ids >> 8) - origin) & (CELLS - 1)
        first_ref[rows, :] = (first - 256).astype(jnp.float32)
        second_ref[rows, :] = (ids & 255).astype(jnp.float32)
        mass_ref[rows, :] = masses
    one_hot_sum(acc_ref, first_ref, second_ref, mass_ref, ROWS)
    blank = jnp.zeros((STRIP, LANES), jnp.float32)
    for r in range(1, quarters):
        quarter = (here + r) & (quarters - 1)
        at = STRIP + (r - 1) * share
        before = jnp.where(quarter == 0, blank, acc_ref[at - STRIP : at, LANES:])
        after = jnp.where(quarter == quarters - 1, blank, acc_ref[at + share : at + share + STRIP, :LANES])
        rows = pl.ds(pl.multiple_of(quarter * STRIP, STRIP), STRIP)
        store_strip(out_ref, rows, acc_ref, at, before, after)
    out_ref[pl.ds(pl.multiple_of(here * STRIP, STRIP), STRIP), :] = jnp.zeros(
        (STRIP, out_ref.shape[1]), jnp.bfloat16
    )
    last = STRIP + (quarters - 1) * share
    side_ref[:STRIP, :] = jnp.where(here == 0, blank, acc_ref[last - STRIP : last, LANES:])
    side_ref[STRIP:, :] = jnp.where(here == quarters - 1, blank, acc_ref[STRIP : 2 * STRIP, :LANES])


def own_kernel(first_ref, second_ref, mass_ref, side_ref, out_ref, moved_ref, acc_ref):
    moved = first_ref[...] + float(acc_ref.shape[0] - STRIP)
    moved_ref[...] = jnp.where(moved < CELLS // 2, moved, moved - CELLS)
    one_hot_sum(acc_ref, moved_ref, second_ref, mass_ref, OWN_ROWS)
    before = side_ref[:STRIP, :]
    after = side_ref[STRIP:, :]
    store_strip(out_ref, pl.ds(0, STRIP), acc_ref, 0, before, after)


def band_kernel(parity_ref, kernel_ref, band_ref, odd_ref):
    parity = parity_ref[0]
    row = lax.broadcasted_iota(jnp.int32, (STRIP, 3 * TERM), 0)
    lane = lax.broadcasted_iota(jnp.int32, (STRIP, 3 * TERM), 1)
    source = lane % TERM
    near = source - PARTS
    far = near - HALO
    near = near + (1 - parity) * (STRIP + HALO)
    far = far + parity * (STRIP + HALO)
    framed = jnp.where(
        source < PARTS,
        HALO + source % STRIP,
        jnp.where(source < PARTS + HALO, near, far),
    )
    tap = framed - row
    for b in range(TAPS):
        whole = jnp.zeros(tap.shape, jnp.float32)
        for a in range(TAPS):
            whole = jnp.where(tap == a, kernel_ref[a, b], whole)
        high = whole.astype(jnp.bfloat16).astype(jnp.float32)
        rest = whole - high
        middle = rest.astype(jnp.bfloat16).astype(jnp.float32)
        term = jnp.where(lane < TERM, high, jnp.where(lane < 2 * TERM, middle, rest - middle))
        band_ref[pl.ds(b * STRIP, STRIP), :] = term
    odd_ref[...] = jnp.broadcast_to(parity.astype(jnp.float32), odd_ref.shape)


def edge_kernel(odd_ref, parts_ref, own_ref, edge_ref, *, top_if_odd):
    is_top = (odd_ref[:HALO, :] > 0.5) == top_if_odd
    for t in range(parts_ref.shape[1] // LANES):
        here = slice(t * LANES, (t + 1) * LANES)
        total = own_ref[:, here].astype(jnp.float32)
        for g in range(parts_ref.shape[0] // STRIP):
            total = total + parts_ref[g * STRIP : (g + 1) * STRIP, here].astype(jnp.float32)
        edge_ref[:, here] = jnp.where(is_top, total[:HALO], total[HALO:]).astype(jnp.bfloat16)


def smooth_kernel(band_ref, parts_ref, own_ref, near_ref, far_ref, out_ref):
    width = parts_ref.shape[1]
    near = near_ref[...].astype(jnp.float32)
    far = far_ref[...].astype(jnp.float32)
    rest = jnp.concatenate([own_ref[...].astype(jnp.float32), near, far], axis=0)
    frame = jnp.concatenate([parts_ref[...], rest.astype(jnp.bfloat16)], axis=0)
    frame = jnp.concatenate([frame, frame, frame], axis=0)
    shifted = jnp.dot(band_ref[...].astype(jnp.bfloat16), frame, preferred_element_type=jnp.float32)
    total = shifted[HALO * STRIP : (HALO + 1) * STRIP]
    for b in range(TAPS):
        if b != HALO:
            part = shifted[b * STRIP : (b + 1) * STRIP]
            total = total + pltpu.roll(part, (HALO - b) % width, 1)
    out_ref[...] = total[:, : out_ref.shape[1]]


def per_device(tile_row, pixel_col, weight, counts, kernel):
    owners = lax.axis_size("own")
    groups = lax.axis_size("grp")
    points = tile_row.shape[2] // LANES
    quarter = W // groups
    width = quarter + LANES
    packed = pl.pallas_call(
        pack_kernel,
        out_shape=jax.ShapeDtypeStruct((3 * owners, LANES), jnp.float32),
        in_specs=[pl.BlockSpec(memory_space=pltpu.HBM)] * 4,
        out_specs=vmem_spec(),
        scratch_shapes=[
            pltpu.VMEM((points, LANES), jnp.int32),
            pltpu.VMEM((points, LANES), jnp.int32),
            pltpu.VMEM((points, 1, LANES), jnp.bfloat16),
            pltpu.VMEM((1, owners), jnp.int32),
            pltpu.VMEM((points, LANES), jnp.float32),
            pltpu.SemaphoreType.DMA((4,)),
        ],
        compiler_params=limit(4),
        name="pack",
    )(
        *(
            pltpu.with_memory_space_constraint(value.reshape(shape), pltpu.HBM)
            for value, shape in (
                (tile_row, (points, LANES)),
                (pixel_col, (points, LANES)),
                (weight, (points, 1, LANES)),
                (counts, (1, owners)),
            )
        )
    )
    arrived = lax.all_to_all(
        packed.reshape(3 * owners, 1, LANES), "own", split_axis=0, concat_axis=0, tiled=True
    ).reshape(3 * owners, LANES)
    plane = jax.ShapeDtypeStruct((points, LANES), jnp.float32)
    sent, side, first, second, mass = pl.pallas_call(
        others_kernel,
        out_shape=(
            jax.ShapeDtypeStruct((groups * STRIP, width), jnp.bfloat16),
            jax.ShapeDtypeStruct((2 * STRIP, LANES), jnp.float32),
            plane,
            plane,
            plane,
        ),
        in_specs=[vmem_spec()],
        out_specs=(vmem_spec(),) * 5,
        scratch_shapes=[pltpu.VMEM((CELLS - CELLS // groups + 2 * STRIP, SPAN), jnp.float32)],
        compiler_params=limit(32),
        name="others",
    )(arrived)
    sent, kernel = lax.optimization_barrier((sent, kernel))
    parts = lax.all_to_all(sent, "grp", split_axis=0, concat_axis=0, tiled=True)
    own = pl.pallas_call(
        own_kernel,
        out_shape=jax.ShapeDtypeStruct((STRIP, width), jnp.bfloat16),
        in_specs=[vmem_spec()] * 4,
        out_specs=vmem_spec(),
        scratch_shapes=[
            pltpu.VMEM((points, LANES), jnp.float32),
            pltpu.VMEM((CELLS // groups, SPAN), jnp.float32),
        ],
        compiler_params=limit(32),
        cost_estimate=pl.CostEstimate(flops=2 * points * LANES * W * STRIP // groups, bytes_accessed=2**19, transcendentals=0),
        name="own",
    )(first, second, mass, side)
    parity = (lax.axis_index("own") & 1).reshape(1).astype(jnp.int32)
    band, odd = pl.pallas_call(
        band_kernel,
        out_shape=(
            jax.ShapeDtypeStruct((TAPS * STRIP, 3 * TERM), jnp.float32),
            jax.ShapeDtypeStruct((STRIP, LANES), jnp.float32),
        ),
        in_specs=[smem_spec(), smem_spec()],
        out_specs=(vmem_spec(),) * 2,
        compiler_params=limit(4),
        name="band",
    )(parity, kernel)
    def edge(parts, top_if_odd, name):
        return pl.pallas_call(
            functools.partial(edge_kernel, top_if_odd=top_if_odd),
            out_shape=jax.ShapeDtypeStruct((HALO, width), jnp.bfloat16),
            in_specs=[vmem_spec()] * 3,
            out_specs=vmem_spec(),
            compiler_params=limit(4),
            name=name,
        )(odd, parts, own)

    near = edge(parts, True, "near")
    near, later = lax.optimization_barrier((near, parts))
    far = edge(later, False, "far")
    on_chip = [(i, i ^ 1) for i in range(owners)]
    across = [(i, i + 1) for i in range(1, owners - 1, 2)]
    across = across + [(j, i) for i, j in across]
    far = lax.ppermute(far, "own", across)
    near = lax.ppermute(near, "own", on_chip)
    return pl.pallas_call(
        smooth_kernel,
        out_shape=jax.ShapeDtypeStruct((STRIP, quarter), jnp.float32),
        in_specs=[vmem_spec()] * 5,
        out_specs=vmem_spec(),
        compiler_params=limit(16),
        name="smooth",
    )(band, parts, own, near, far)


def solution(mesh):
    placed = (
        P("grp", "own", None),
        P("grp", "own", None),
        P("grp", "own", None),
        P("grp", "own", None),
        P(),
    )
    return jax.shard_map(
        per_device, mesh=mesh, in_specs=placed, out_specs=P("own", "grp"), check_vma=False
    )
```

```python
import functools

import jax
import jax.numpy as jnp
from jax import lax
from jax.experimental import pallas as pl
from jax.experimental.pallas import tpu as pltpu
from jax.sharding import PartitionSpec as P

W = 16384
STRIP = 8
CAP = 192
LANES = 128
HALO = 4
TAPS = 2 * HALO + 1
PARTS = 40
TERM = 48
SPAN = 256
CELLS = STRIP * W // SPAN
ROWS = 96
OWN_ROWS = 96


def vmem_spec():
    return pl.BlockSpec(memory_space=pltpu.VMEM)


def smem_spec():
    return pl.BlockSpec(memory_space=pltpu.SMEM)


def limit(mebibytes):
    return pltpu.CompilerParams(vmem_limit_bytes=mebibytes * 2**20)


def pack_kernel(row_in, col_in, weight_in, count_in, out_ref, row_ref, col_ref, weight_ref, count_ref, wide_ref, sems):
    copies = [
        pltpu.make_async_copy(source, target, sems.at[i])
        for i, (source, target) in enumerate(
            ((weight_in, weight_ref), (count_in, count_ref), (row_in, row_ref), (col_in, col_ref))
        )
    ]
    for copy in copies:
        copy.start()
    for copy in copies:
        copy.wait()
    points = row_ref.shape[0]
    pairs = points // 3
    for i in range(points):
        wide_ref[pl.ds(i, 1), :] = weight_ref[i].astype(jnp.float32)
    lane = lax.broadcasted_iota(jnp.int32, (pairs, LANES), 1)
    block = lax.broadcasted_iota(jnp.int32, (pairs, LANES), 0)
    counts = jnp.broadcast_to(count_ref[...], (pairs, LANES))
    even = jnp.sum(jnp.where(lane == 2 * block, counts, 0), axis=1, keepdims=True)
    odd = jnp.sum(jnp.where(lane == 2 * block + 1, counts, 0), axis=1, keepdims=True)
    low = lane < 64
    lives = (
        lane < even,
        jnp.where(low, lane + 128, lane - 64) < jnp.where(low, even, odd),
        lane + 64 < odd,
    )
    ids, masses = [], []
    for k in range(3):
        tile_row = row_ref[pl.ds(k, pairs, stride=3), :]
        column = col_ref[pl.ds(k, pairs, stride=3), :]
        index = (((column >> 8) * STRIP + tile_row) << 8) + (column & 255)
        ids.append(index.astype(jnp.float32))
        masses.append(jnp.where(lives[k], wide_ref[pl.ds(k, pairs, stride=3), :], 0.0))
    half = LANES // 2
    out_ref[pl.ds(0, pairs, stride=6), :] = ids[0]
    out_ref[pl.ds(1, pairs, stride=6), :] = jnp.where(low, ids[1], pltpu.roll(masses[1], half, 1))
    out_ref[pl.ds(2, pairs, stride=6), :] = masses[0]
    out_ref[pl.ds(3, pairs, stride=6), :] = ids[2]
    out_ref[pl.ds(4, pairs, stride=6), :] = jnp.where(low, pltpu.roll(ids[1], half, 1), masses[1])
    out_ref[pl.ds(5, pairs, stride=6), :] = masses[2]


def one_hot_sum(acc_ref, first_ref, second_ref, mass_ref, rows):
    cells = acc_ref.shape[0]
    first_iota = (
        lax.broadcasted_iota(jnp.int32, (cells, LANES), 0).astype(jnp.float32) - 256.0
    ).astype(jnp.bfloat16)
    second_iota = lax.broadcasted_iota(jnp.int32, (SPAN, LANES), 0).astype(jnp.float32).astype(jnp.bfloat16)
    one = jnp.ones((), jnp.bfloat16)
    zero = jnp.zeros((), jnp.bfloat16)
    acc_ref[...] = jnp.zeros_like(acc_ref)

    def step(i, carry):
        here = pl.ds(pl.multiple_of(i * rows, rows), rows)
        first = first_ref[here, :].astype(jnp.bfloat16)
        second = second_ref[here, :].astype(jnp.bfloat16)
        mass = mass_ref[here, :].astype(jnp.bfloat16)
        left, right = [], []
        for r in range(rows):
            left.append(jnp.where(first_iota == first[r : r + 1], one, zero))
            right.append(jnp.where(second_iota == second[r : r + 1], mass[r : r + 1], zero))
        acc_ref[...] += lax.dot_general(
            jnp.concatenate(left, axis=1),
            jnp.concatenate(right, axis=1),
            (((1,), (1,)), ((), ())),
            preferred_element_type=jnp.float32,
        )
        return carry

    lax.fori_loop(0, first_ref.shape[0] // rows, step, 0)


def store_strip(out_ref, rows, acc_ref, at, before, after):
    span = out_ref.shape[1] - LANES
    for c in range(span // SPAN):
        block = acc_ref[at + c * STRIP : at + (c + 1) * STRIP, :]
        out_ref[rows, c * SPAN : (c + 1) * SPAN] = block.astype(jnp.bfloat16)
    low = lax.broadcasted_iota(jnp.int32, (STRIP, LANES), 1) < 64
    out_ref[rows, span:] = jnp.where(low, after, before).astype(jnp.bfloat16)


def others_kernel(points_ref, out_ref, side_ref, first_ref, second_ref, mass_ref, acc_ref):
    quarters = out_ref.shape[0] // STRIP
    here = lax.axis_index("grp")
    share = CELLS // quarters
    sources = points_ref.shape[0] // 3
    half = sources // 2
    low = lax.broadcasted_iota(jnp.int32, (half, LANES), 1) < 64
    upper = points_ref[pl.ds(1, half, stride=3), :]
    lower = points_ref[pl.ds(1 + 3 * half, half, stride=3), :]
    mixed_ids = jnp.where(low, upper, pltpu.roll(lower, 64, 1))
    mixed_masses = jnp.where(low, pltpu.roll(upper, 64, 1), lower)
    origin = (here + 1) * share - STRIP
    for ids, masses, at in (
        (points_ref[pl.ds(0, sources, stride=3), :], points_ref[pl.ds(2, sources, stride=3), :], 0),
        (mixed_ids, mixed_masses, sources),
    ):
        ids = ids.astype(jnp.int32)
        rows = pl.ds(at, ids.shape[0])
        first = ((ids >> 8) - origin) & (CELLS - 1)
        first_ref[rows, :] = (first - 256).astype(jnp.float32)
        second_ref[rows, :] = (ids & 255).astype(jnp.float32)
        mass_ref[rows, :] = masses
    one_hot_sum(acc_ref, first_ref, second_ref, mass_ref, ROWS)
    blank = jnp.zeros((STRIP, LANES), jnp.float32)
    for r in range(1, quarters):
        quarter = (here + r) & (quarters - 1)
        at = STRIP + (r - 1) * share
        before = jnp.where(quarter == 0, blank, acc_ref[at - STRIP : at, LANES:])
        after = jnp.where(quarter == quarters - 1, blank, acc_ref[at + share : at + share + STRIP, :LANES])
        rows = pl.ds(pl.multiple_of(quarter * STRIP, STRIP), STRIP)
        store_strip(out_ref, rows, acc_ref, at, before, after)
    out_ref[pl.ds(pl.multiple_of(here * STRIP, STRIP), STRIP), :] = jnp.zeros(
        (STRIP, out_ref.shape[1]), jnp.bfloat16
    )
    last = STRIP + (quarters - 1) * share
    side_ref[:STRIP, :] = jnp.where(here == 0, blank, acc_ref[last - STRIP : last, LANES:])
    side_ref[STRIP:, :] = jnp.where(here == quarters - 1, blank, acc_ref[STRIP : 2 * STRIP, :LANES])


def own_kernel(first_ref, second_ref, mass_ref, side_ref, out_ref, moved_ref, acc_ref):
    moved = first_ref[...] + float(acc_ref.shape[0] - STRIP)
    moved_ref[...] = jnp.where(moved < CELLS // 2, moved, moved - CELLS)
    one_hot_sum(acc_ref, moved_ref, second_ref, mass_ref, OWN_ROWS)
    before = side_ref[:STRIP, :]
    after = side_ref[STRIP:, :]
    store_strip(out_ref, pl.ds(0, STRIP), acc_ref, 0, before, after)


def band_kernel(parity_ref, kernel_ref, band_ref, odd_ref):
    parity = parity_ref[0]
    row = lax.broadcasted_iota(jnp.int32, (STRIP, 3 * TERM), 0)
    lane = lax.broadcasted_iota(jnp.int32, (STRIP, 3 * TERM), 1)
    source = lane % TERM
    near = source - PARTS
    far = near - HALO
    near = near + (1 - parity) * (STRIP + HALO)
    far = far + parity * (STRIP + HALO)
    framed = jnp.where(
        source < PARTS,
        HALO + source % STRIP,
        jnp.where(source < PARTS + HALO, near, far),
    )
    tap = framed - row
    for b in range(TAPS):
        whole = jnp.zeros(tap.shape, jnp.float32)
        for a in range(TAPS):
            whole = jnp.where(tap == a, kernel_ref[a, b], whole)
        high = whole.astype(jnp.bfloat16).astype(jnp.float32)
        rest = whole - high
        middle = rest.astype(jnp.bfloat16).astype(jnp.float32)
        term = jnp.where(lane < TERM, high, jnp.where(lane < 2 * TERM, middle, rest - middle))
        band_ref[pl.ds(b * STRIP, STRIP), :] = term
    odd_ref[...] = jnp.broadcast_to(parity.astype(jnp.float32), odd_ref.shape)


def edge_kernel(odd_ref, parts_ref, own_ref, edge_ref, *, top_if_odd):
    is_top = (odd_ref[:HALO, :] > 0.5) == top_if_odd
    for t in range(parts_ref.shape[1] // LANES):
        here = slice(t * LANES, (t + 1) * LANES)
        total = own_ref[:, here].astype(jnp.float32)
        for g in range(parts_ref.shape[0] // STRIP):
            total = total + parts_ref[g * STRIP : (g + 1) * STRIP, here].astype(jnp.float32)
        edge_ref[:, here] = jnp.where(is_top, total[:HALO], total[HALO:]).astype(jnp.bfloat16)


def smooth_kernel(band_ref, parts_ref, own_ref, near_ref, far_ref, out_ref):
    width = parts_ref.shape[1]
    near = near_ref[...].astype(jnp.float32)
    far = far_ref[...].astype(jnp.float32)
    rest = jnp.concatenate([own_ref[...].astype(jnp.float32), near, far], axis=0)
    frame = jnp.concatenate([parts_ref[...], rest.astype(jnp.bfloat16)], axis=0)
    frame = jnp.concatenate([frame, frame, frame], axis=0)
    shifted = jnp.dot(band_ref[...].astype(jnp.bfloat16), frame, preferred_element_type=jnp.float32)
    total = shifted[HALO * STRIP : (HALO + 1) * STRIP]
    for b in range(TAPS):
        if b != HALO:
            part = shifted[b * STRIP : (b + 1) * STRIP]
            total = total + pltpu.roll(part, (HALO - b) % width, 1)
    out_ref[...] = total[:, : out_ref.shape[1]]


def per_device(tile_row, pixel_col, weight, counts, kernel):
    owners = lax.axis_size("own")
    groups = lax.axis_size("grp")
    points = tile_row.shape[2] // LANES
    quarter = W // groups
    width = quarter + LANES
    packed = pl.pallas_call(
        pack_kernel,
        out_shape=jax.ShapeDtypeStruct((3 * owners, LANES), jnp.float32),
        in_specs=[pl.BlockSpec(memory_space=pltpu.HBM)] * 4,
        out_specs=vmem_spec(),
        scratch_shapes=[
            pltpu.VMEM((points, LANES), jnp.int32),
            pltpu.VMEM((points, LANES), jnp.int32),
            pltpu.VMEM((points, 1, LANES), jnp.bfloat16),
            pltpu.VMEM((1, owners), jnp.int32),
            pltpu.VMEM((points, LANES), jnp.float32),
            pltpu.SemaphoreType.DMA((4,)),
        ],
        compiler_params=limit(4),
        name="pack",
    )(
        *(
            pltpu.with_memory_space_constraint(value.reshape(shape), pltpu.HBM)
            for value, shape in (
                (tile_row, (points, LANES)),
                (pixel_col, (points, LANES)),
                (weight, (points, 1, LANES)),
                (counts, (1, owners)),
            )
        )
    )
    packed, kernel = lax.optimization_barrier((packed, kernel))
    arrived = lax.all_to_all(
        packed.reshape(3 * owners, 1, LANES), "own", split_axis=0, concat_axis=0, tiled=True
    ).reshape(3 * owners, LANES)
    parity = (lax.axis_index("own") & 1).reshape(1).astype(jnp.int32)
    band, odd = pl.pallas_call(
        band_kernel,
        out_shape=(
            jax.ShapeDtypeStruct((TAPS * STRIP, 3 * TERM), jnp.float32),
            jax.ShapeDtypeStruct((STRIP, LANES), jnp.float32),
        ),
        in_specs=[smem_spec(), smem_spec()],
        out_specs=(vmem_spec(),) * 2,
        compiler_params=limit(4),
        name="band",
    )(parity, kernel)
    arrived, band, odd = lax.optimization_barrier((arrived, band, odd))
    plane = jax.ShapeDtypeStruct((points, LANES), jnp.float32)
    sent, side, first, second, mass = pl.pallas_call(
        others_kernel,
        out_shape=(
            jax.ShapeDtypeStruct((groups * STRIP, width), jnp.bfloat16),
            jax.ShapeDtypeStruct((2 * STRIP, LANES), jnp.float32),
            plane,
            plane,
            plane,
        ),
        in_specs=[vmem_spec()],
        out_specs=(vmem_spec(),) * 5,
        scratch_shapes=[pltpu.VMEM((CELLS - CELLS // groups + 2 * STRIP, SPAN), jnp.float32)],
        compiler_params=limit(32),
        name="others",
    )(arrived)
    parts = lax.all_to_all(sent, "grp", split_axis=0, concat_axis=0, tiled=True)
    own = pl.pallas_call(
        own_kernel,
        out_shape=jax.ShapeDtypeStruct((STRIP, width), jnp.bfloat16),
        in_specs=[vmem_spec()] * 4,
        out_specs=vmem_spec(),
        scratch_shapes=[
            pltpu.VMEM((points, LANES), jnp.float32),
            pltpu.VMEM((CELLS // groups, SPAN), jnp.float32),
        ],
        compiler_params=limit(32),
        cost_estimate=pl.CostEstimate(flops=2 * points * LANES * W * STRIP // groups, bytes_accessed=2**19, transcendentals=0),
        name="own",
    )(first, second, mass, side)
    def edge(parts, top_if_odd, name):
        return pl.pallas_call(
            functools.partial(edge_kernel, top_if_odd=top_if_odd),
            out_shape=jax.ShapeDtypeStruct((HALO, width), jnp.bfloat16),
            in_specs=[vmem_spec()] * 3,
            out_specs=vmem_spec(),
            compiler_params=limit(4),
            name=name,
        )(odd, parts, own)

    near = edge(parts, True, "near")
    near, later = lax.optimization_barrier((near, parts))
    far = edge(later, False, "far")
    on_chip = [(i, i ^ 1) for i in range(owners)]
    across = [(i, i + 1) for i in range(1, owners - 1, 2)]
    across = across + [(j, i) for i, j in across]
    far = lax.ppermute(far, "own", across)
    near = lax.ppermute(near, "own", on_chip)
    return pl.pallas_call(
        smooth_kernel,
        out_shape=jax.ShapeDtypeStruct((STRIP, quarter), jnp.float32),
        in_specs=[vmem_spec()] * 5,
        out_specs=vmem_spec(),
        compiler_params=limit(16),
        name="smooth",
    )(band, parts, own, near, far)


def solution(mesh):
    placed = (
        P("grp", "own", None),
        P("grp", "own", None),
        P("grp", "own", None),
        P("grp", "own", None),
        P(),
    )
    return jax.shard_map(
        per_device, mesh=mesh, in_specs=placed, out_specs=P("own", "grp"), check_vma=False
    )
```

```python
import functools

import jax
import jax.numpy as jnp
from jax import lax
from jax.experimental import pallas as pl
from jax.experimental.pallas import tpu as pltpu
from jax.sharding import PartitionSpec as P

W = 16384
STRIP = 8
CAP = 192
LANES = 128
HALO = 4
TAPS = 2 * HALO + 1
PARTS = 40
TERM = 48
SPAN = 256
CELLS = STRIP * W // SPAN
ROWS = 96
OWN_ROWS = 96


def vmem_spec():
    return pl.BlockSpec(memory_space=pltpu.VMEM)


def smem_spec():
    return pl.BlockSpec(memory_space=pltpu.SMEM)


def limit(mebibytes):
    return pltpu.CompilerParams(vmem_limit_bytes=mebibytes * 2**20)


def pack_kernel(row_in, col_in, weight_in, count_in, out_ref, row_ref, col_ref, weight_ref, count_ref, wide_ref, sems):
    copies = [
        pltpu.make_async_copy(source, target, sems.at[i])
        for i, (source, target) in enumerate(
            ((weight_in, weight_ref), (count_in, count_ref), (row_in, row_ref), (col_in, col_ref))
        )
    ]
    for copy in copies:
        copy.start()
    for copy in copies:
        copy.wait()
    points = row_ref.shape[0]
    pairs = points // 3
    for i in range(points):
        wide_ref[pl.ds(i, 1), :] = weight_ref[i].astype(jnp.float32)
    lane = lax.broadcasted_iota(jnp.int32, (pairs, LANES), 1)
    block = lax.broadcasted_iota(jnp.int32, (pairs, LANES), 0)
    counts = jnp.broadcast_to(count_ref[...], (pairs, LANES))
    even = jnp.sum(jnp.where(lane == 2 * block, counts, 0), axis=1, keepdims=True)
    odd = jnp.sum(jnp.where(lane == 2 * block + 1, counts, 0), axis=1, keepdims=True)
    low = lane < 64
    lives = (
        lane < even,
        jnp.where(low, lane + 128, lane - 64) < jnp.where(low, even, odd),
        lane + 64 < odd,
    )
    ids, masses = [], []
    for k in range(3):
        tile_row = row_ref[pl.ds(k, pairs, stride=3), :]
        column = col_ref[pl.ds(k, pairs, stride=3), :]
        index = (((column >> 8) * STRIP + tile_row) << 8) + (column & 255)
        ids.append(index.astype(jnp.float32))
        masses.append(jnp.where(lives[k], wide_ref[pl.ds(k, pairs, stride=3), :], 0.0))
    half = LANES // 2
    out_ref[pl.ds(0, pairs, stride=6), :] = ids[0]
    out_ref[pl.ds(1, pairs, stride=6), :] = jnp.where(low, ids[1], pltpu.roll(masses[1], half, 1))
    out_ref[pl.ds(2, pairs, stride=6), :] = masses[0]
    out_ref[pl.ds(3, pairs, stride=6), :] = ids[2]
    out_ref[pl.ds(4, pairs, stride=6), :] = jnp.where(low, pltpu.roll(ids[1], half, 1), masses[1])
    out_ref[pl.ds(5, pairs, stride=6), :] = masses[2]


def one_hot_sum(acc_ref, first_ref, second_ref, mass_ref, rows):
    cells = acc_ref.shape[0]
    first_iota = (
        lax.broadcasted_iota(jnp.int32, (cells, LANES), 0).astype(jnp.float32) - 256.0
    ).astype(jnp.bfloat16)
    second_iota = lax.broadcasted_iota(jnp.int32, (SPAN, LANES), 0).astype(jnp.float32).astype(jnp.bfloat16)
    one = jnp.ones((), jnp.bfloat16)
    zero = jnp.zeros((), jnp.bfloat16)

    def part(i):
        here = pl.ds(i * rows, rows)
        first = first_ref[here, :].astype(jnp.bfloat16)
        second = second_ref[here, :].astype(jnp.bfloat16)
        mass = mass_ref[here, :].astype(jnp.bfloat16)
        left, right = [], []
        for r in range(rows):
            left.append(jnp.where(first_iota == first[r : r + 1], one, zero))
            right.append(jnp.where(second_iota == second[r : r + 1], mass[r : r + 1], zero))
        return lax.dot_general(
            jnp.concatenate(left, axis=1),
            jnp.concatenate(right, axis=1),
            (((1,), (1,)), ((), ())),
            preferred_element_type=jnp.float32,
        )

    acc_ref[...] = part(0)
    for i in range(1, first_ref.shape[0] // rows):
        acc_ref[...] += part(i)


def store_strip(out_ref, rows, acc_ref, at, before, after):
    span = out_ref.shape[1] - LANES
    for c in range(span // SPAN):
        block = acc_ref[at + c * STRIP : at + (c + 1) * STRIP, :]
        out_ref[rows, c * SPAN : (c + 1) * SPAN] = block.astype(jnp.bfloat16)
    low = lax.broadcasted_iota(jnp.int32, (STRIP, LANES), 1) < 64
    out_ref[rows, span:] = jnp.where(low, after, before).astype(jnp.bfloat16)


def others_kernel(points_ref, out_ref, side_ref, first_ref, second_ref, mass_ref, acc_ref):
    quarters = out_ref.shape[0] // STRIP
    here = lax.axis_index("grp")
    share = CELLS // quarters
    sources = points_ref.shape[0] // 3
    half = sources // 2
    low = lax.broadcasted_iota(jnp.int32, (half, LANES), 1) < 64
    upper = points_ref[pl.ds(1, half, stride=3), :]
    lower = points_ref[pl.ds(1 + 3 * half, half, stride=3), :]
    mixed_ids = jnp.where(low, upper, pltpu.roll(lower, 64, 1))
    mixed_masses = jnp.where(low, pltpu.roll(upper, 64, 1), lower)
    origin = (here + 1) * share - STRIP
    for ids, masses, at in (
        (points_ref[pl.ds(0, sources, stride=3), :], points_ref[pl.ds(2, sources, stride=3), :], 0),
        (mixed_ids, mixed_masses, sources),
    ):
        ids = ids.astype(jnp.int32)
        rows = pl.ds(at, ids.shape[0])
        first = ((ids >> 8) - origin) & (CELLS - 1)
        first_ref[rows, :] = (first - 256).astype(jnp.float32)
        second_ref[rows, :] = (ids & 255).astype(jnp.float32)
        mass_ref[rows, :] = masses
    one_hot_sum(acc_ref, first_ref, second_ref, mass_ref, ROWS)
    blank = jnp.zeros((STRIP, LANES), jnp.float32)
    for r in range(1, quarters):
        quarter = (here + r) & (quarters - 1)
        at = STRIP + (r - 1) * share
        before = jnp.where(quarter == 0, blank, acc_ref[at - STRIP : at, LANES:])
        after = jnp.where(quarter == quarters - 1, blank, acc_ref[at + share : at + share + STRIP, :LANES])
        rows = pl.ds(pl.multiple_of(quarter * STRIP, STRIP), STRIP)
        store_strip(out_ref, rows, acc_ref, at, before, after)
    out_ref[pl.ds(pl.multiple_of(here * STRIP, STRIP), STRIP), :] = jnp.zeros(
        (STRIP, out_ref.shape[1]), jnp.bfloat16
    )
    last = STRIP + (quarters - 1) * share
    side_ref[:STRIP, :] = jnp.where(here == 0, blank, acc_ref[last - STRIP : last, LANES:])
    side_ref[STRIP:, :] = jnp.where(here == quarters - 1, blank, acc_ref[STRIP : 2 * STRIP, :LANES])


def own_kernel(first_ref, second_ref, mass_ref, side_ref, out_ref, moved_ref, acc_ref):
    moved = first_ref[...] + float(out_ref.shape[1] // SPAN * STRIP - STRIP)
    moved_ref[...] = jnp.where(moved < CELLS // 2, moved, moved - CELLS)
    one_hot_sum(acc_ref, moved_ref, second_ref, mass_ref, OWN_ROWS)
    before = side_ref[:STRIP, :]
    after = side_ref[STRIP:, :]
    store_strip(out_ref, pl.ds(0, STRIP), acc_ref, 0, before, after)


def band_kernel(parity_ref, kernel_ref, band_ref, odd_ref):
    parity = parity_ref[0]
    row = lax.broadcasted_iota(jnp.int32, (STRIP, 3 * TERM), 0)
    lane = lax.broadcasted_iota(jnp.int32, (STRIP, 3 * TERM), 1)
    source = lane % TERM
    near = source - PARTS
    far = near - HALO
    near = near + (1 - parity) * (STRIP + HALO)
    far = far + parity * (STRIP + HALO)
    framed = jnp.where(
        source < PARTS,
        HALO + source % STRIP,
        jnp.where(source < PARTS + HALO, near, far),
    )
    tap = framed - row
    for b in range(TAPS):
        whole = jnp.zeros(tap.shape, jnp.float32)
        for a in range(TAPS):
            whole = jnp.where(tap == a, kernel_ref[a, b], whole)
        high = whole.astype(jnp.bfloat16).astype(jnp.float32)
        rest = whole - high
        middle = rest.astype(jnp.bfloat16).astype(jnp.float32)
        term = jnp.where(lane < TERM, high, jnp.where(lane < 2 * TERM, middle, rest - middle))
        band_ref[pl.ds(b * STRIP, STRIP), :] = term
    odd_ref[...] = jnp.broadcast_to(parity.astype(jnp.float32), odd_ref.shape)


def edge_kernel(odd_ref, parts_ref, own_ref, edge_ref, *, top_if_odd):
    is_top = (odd_ref[:HALO, :] > 0.5) == top_if_odd
    for t in range(parts_ref.shape[1] // LANES):
        here = slice(t * LANES, (t + 1) * LANES)
        total = own_ref[:, here].astype(jnp.float32)
        for g in range(parts_ref.shape[0] // STRIP):
            total = total + parts_ref[g * STRIP : (g + 1) * STRIP, here].astype(jnp.float32)
        edge_ref[:, here] = jnp.where(is_top, total[:HALO], total[HALO:]).astype(jnp.bfloat16)


def smooth_kernel(band_ref, parts_ref, own_ref, near_ref, far_ref, out_ref):
    width = parts_ref.shape[1]
    near = near_ref[...].astype(jnp.float32)
    far = far_ref[...].astype(jnp.float32)
    rest = jnp.concatenate([own_ref[...].astype(jnp.float32), near, far], axis=0)
    frame = jnp.concatenate([parts_ref[...], rest.astype(jnp.bfloat16)], axis=0)
    frame = jnp.concatenate([frame, frame, frame], axis=0)
    shifted = jnp.dot(band_ref[...].astype(jnp.bfloat16), frame, preferred_element_type=jnp.float32)
    total = shifted[HALO * STRIP : (HALO + 1) * STRIP]
    for b in range(TAPS):
        if b != HALO:
            part = shifted[b * STRIP : (b + 1) * STRIP]
            total = total + pltpu.roll(part, (HALO - b) % width, 1)
    out_ref[...] = total[:, : out_ref.shape[1]]


def per_device(tile_row, pixel_col, weight, counts, kernel):
    owners = lax.axis_size("own")
    groups = lax.axis_size("grp")
    points = tile_row.shape[2] // LANES
    quarter = W // groups
    width = quarter + LANES
    packed = pl.pallas_call(
        pack_kernel,
        out_shape=jax.ShapeDtypeStruct((3 * owners, LANES), jnp.float32),
        in_specs=[pl.BlockSpec(memory_space=pltpu.HBM)] * 4,
        out_specs=vmem_spec(),
        scratch_shapes=[
            pltpu.VMEM((points, LANES), jnp.int32),
            pltpu.VMEM((points, LANES), jnp.int32),
            pltpu.VMEM((points, 1, LANES), jnp.bfloat16),
            pltpu.VMEM((1, owners), jnp.int32),
            pltpu.VMEM((points, LANES), jnp.float32),
            pltpu.SemaphoreType.DMA((4,)),
        ],
        compiler_params=limit(4),
        name="pack",
    )(
        *(
            pltpu.with_memory_space_constraint(value.reshape(shape), pltpu.HBM)
            for value, shape in (
                (tile_row, (points, LANES)),
                (pixel_col, (points, LANES)),
                (weight, (points, 1, LANES)),
                (counts, (1, owners)),
            )
        )
    )
    arrived = lax.all_to_all(
        packed.reshape(3 * owners, 1, LANES), "own", split_axis=0, concat_axis=0, tiled=True
    ).reshape(3 * owners, LANES)
    plane = jax.ShapeDtypeStruct((points, LANES), jnp.float32)
    sent, side, first, second, mass = pl.pallas_call(
        others_kernel,
        out_shape=(
            jax.ShapeDtypeStruct((groups * STRIP, width), jnp.bfloat16),
            jax.ShapeDtypeStruct((2 * STRIP, LANES), jnp.float32),
            plane,
            plane,
            plane,
        ),
        in_specs=[vmem_spec()],
        out_specs=(vmem_spec(),) * 5,
        scratch_shapes=[pltpu.VMEM((CELLS - CELLS // groups + 2 * STRIP, SPAN), jnp.float32)],
        compiler_params=limit(32),
        name="others",
    )(arrived)
    sent, kernel = lax.optimization_barrier((sent, kernel))
    parts = lax.all_to_all(sent, "grp", split_axis=0, concat_axis=0, tiled=True)
    own = pl.pallas_call(
        own_kernel,
        out_shape=jax.ShapeDtypeStruct((STRIP, width), jnp.bfloat16),
        in_specs=[vmem_spec()] * 4,
        out_specs=vmem_spec(),
        scratch_shapes=[
            pltpu.VMEM((points, LANES), jnp.float32),
            pltpu.VMEM((max(CELLS // groups, 256), SPAN), jnp.float32),
        ],
        compiler_params=limit(32),
        cost_estimate=pl.CostEstimate(flops=2 * points * LANES * W * STRIP // groups, bytes_accessed=2**19, transcendentals=0),
        name="own",
    )(first, second, mass, side)
    parity = (lax.axis_index("own") & 1).reshape(1).astype(jnp.int32)
    band, odd = pl.pallas_call(
        band_kernel,
        out_shape=(
            jax.ShapeDtypeStruct((TAPS * STRIP, 3 * TERM), jnp.float32),
            jax.ShapeDtypeStruct((STRIP, LANES), jnp.float32),
        ),
        in_specs=[smem_spec(), smem_spec()],
        out_specs=(vmem_spec(),) * 2,
        compiler_params=limit(4),
        name="band",
    )(parity, kernel)
    def edge(parts, top_if_odd, name):
        return pl.pallas_call(
            functools.partial(edge_kernel, top_if_odd=top_if_odd),
            out_shape=jax.ShapeDtypeStruct((HALO, width), jnp.bfloat16),
            in_specs=[vmem_spec()] * 3,
            out_specs=vmem_spec(),
            compiler_params=limit(4),
            name=name,
        )(odd, parts, own)

    near = edge(parts, True, "near")
    near, later = lax.optimization_barrier((near, parts))
    far = edge(later, False, "far")
    on_chip = [(i, i ^ 1) for i in range(owners)]
    across = [(i, i + 1) for i in range(1, owners - 1, 2)]
    across = across + [(j, i) for i, j in across]
    far = lax.ppermute(far, "own", across)
    near = lax.ppermute(near, "own", on_chip)
    return pl.pallas_call(
        smooth_kernel,
        out_shape=jax.ShapeDtypeStruct((STRIP, quarter), jnp.float32),
        in_specs=[vmem_spec()] * 5,
        out_specs=vmem_spec(),
        compiler_params=limit(16),
        name="smooth",
    )(band, parts, own, near, far)


def solution(mesh):
    placed = (
        P("grp", "own", None),
        P("grp", "own", None),
        P("grp", "own", None),
        P("grp", "own", None),
        P(),
    )
    return jax.shard_map(
        per_device, mesh=mesh, in_specs=placed, out_specs=P("own", "grp"), check_vma=False
    )
```

```python
import functools

import jax
import jax.numpy as jnp
from jax import lax
from jax.experimental import pallas as pl
from jax.experimental.pallas import tpu as pltpu
from jax.sharding import PartitionSpec as P

W = 16384
STRIP = 8
CAP = 192
LANES = 128
HALO = 4
TAPS = 2 * HALO + 1
PARTS = 40
TERM = 48
SPAN = 256
CELLS = STRIP * W // SPAN
ROWS = 136
STEP = 8


def vmem_spec():
    return pl.BlockSpec(memory_space=pltpu.VMEM)


def smem_spec():
    return pl.BlockSpec(memory_space=pltpu.SMEM)


def limit(mebibytes):
    return pltpu.CompilerParams(vmem_limit_bytes=mebibytes * 2**20)


def pack_kernel(row_in, col_in, weight_in, count_in, out_ref, row_ref, col_ref, weight_ref, count_ref, wide_ref, sems):
    copies = [
        pltpu.make_async_copy(source, target, sems.at[i])
        for i, (source, target) in enumerate(
            ((weight_in, weight_ref), (count_in, count_ref), (row_in, row_ref), (col_in, col_ref))
        )
    ]
    for copy in copies:
        copy.start()
    for copy in copies:
        copy.wait()
    points = row_ref.shape[0]
    pairs = points // 3
    for i in range(points):
        wide_ref[pl.ds(i, 1), :] = weight_ref[i].astype(jnp.float32)
    lane = lax.broadcasted_iota(jnp.int32, (pairs, LANES), 1)
    block = lax.broadcasted_iota(jnp.int32, (pairs, LANES), 0)
    counts = jnp.broadcast_to(count_ref[...], (pairs, LANES))
    even = jnp.sum(jnp.where(lane == 2 * block, counts, 0), axis=1, keepdims=True)
    odd = jnp.sum(jnp.where(lane == 2 * block + 1, counts, 0), axis=1, keepdims=True)
    low = lane < 64
    lives = (
        lane < even,
        jnp.where(low, lane + 128, lane - 64) < jnp.where(low, even, odd),
        lane + 64 < odd,
    )
    ids, masses = [], []
    for k in range(3):
        tile_row = row_ref[pl.ds(k, pairs, stride=3), :]
        column = col_ref[pl.ds(k, pairs, stride=3), :]
        index = (((column >> 8) * STRIP + tile_row) << 8) + (column & 255)
        ids.append(index.astype(jnp.float32))
        masses.append(jnp.where(lives[k], wide_ref[pl.ds(k, pairs, stride=3), :], 0.0))
    half = LANES // 2
    out_ref[pl.ds(0, pairs, stride=6), :] = ids[0]
    out_ref[pl.ds(1, pairs, stride=6), :] = jnp.where(low, ids[1], pltpu.roll(masses[1], half, 1))
    out_ref[pl.ds(2, pairs, stride=6), :] = masses[0]
    out_ref[pl.ds(3, pairs, stride=6), :] = ids[2]
    out_ref[pl.ds(4, pairs, stride=6), :] = jnp.where(low, pltpu.roll(ids[1], half, 1), masses[1])
    out_ref[pl.ds(5, pairs, stride=6), :] = masses[2]


def one_hot_sum(cells, first_ref, second_ref, mass_ref, start, rows):
    first_iota = (
        lax.broadcasted_iota(jnp.int32, (cells, LANES), 0).astype(jnp.float32) - 256.0
    ).astype(jnp.bfloat16)
    second_iota = lax.broadcasted_iota(jnp.int32, (SPAN, LANES), 0).astype(jnp.float32).astype(jnp.bfloat16)
    one = jnp.ones((), jnp.bfloat16)
    zero = jnp.zeros((), jnp.bfloat16)
    here = pl.ds(start, rows)
    first = first_ref[here, :].astype(jnp.bfloat16)
    second = second_ref[here, :].astype(jnp.bfloat16)
    mass = mass_ref[here, :].astype(jnp.bfloat16)
    left, right = [], []
    for r in range(rows):
        left.append(jnp.where(first_iota == first[r : r + 1], one, zero))
        right.append(jnp.where(second_iota == second[r : r + 1], mass[r : r + 1], zero))
    return lax.dot_general(
        jnp.concatenate(left, axis=1),
        jnp.concatenate(right, axis=1),
        (((1,), (1,)), ((), ())),
        preferred_element_type=jnp.float32,
    )


def packed_units(planes, live):
    units = live.shape[0]
    count = units // 2
    low = lax.broadcasted_iota(jnp.int32, (count, LANES), 1) < 64

    def placed(value, is_high, to_high):
        moved = value if is_high == to_high else pltpu.roll(value, 64, 1)
        return jnp.where(low, 0.0, moved) if to_high else jnp.where(low, moved, 0.0)

    sources = jnp.concatenate(
        [
            jnp.concatenate([placed(value, is_high, to_high) for value, is_high in kind], axis=1)
            for to_high in (False, True)
            for kind in planes
        ],
        axis=0,
    ).astype(jnp.bfloat16)
    row = lax.broadcasted_iota(jnp.int32, (units, units), 0)
    column = lax.broadcasted_iota(jnp.int32, (units, units), 1)
    counted = jnp.where(row < column, 1.0, jnp.where(row == column, 512.0, 0.0))
    counted = (jnp.broadcast_to(live, (units, units)) * counted).astype(jnp.bfloat16)
    place = jnp.dot(jnp.ones((8, units), jnp.bfloat16), counted, preferred_element_type=jnp.float32)
    place = jnp.broadcast_to(place[:1] - 512.0, (count, units))
    target = lax.broadcasted_iota(jnp.int32, (count, units), 0).astype(jnp.float32) * 2.0
    chosen = jnp.concatenate(
        [jnp.where(place == target, 1.0, 0.0), jnp.where(place == target + 1.0, 1.0, 0.0)], axis=1
    ).astype(jnp.bfloat16)
    return jnp.dot(chosen, sources, preferred_element_type=jnp.float32)


def store_strip(out_ref, rows, acc_ref, at, before, after):
    span = out_ref.shape[1] - LANES
    for c in range(span // SPAN):
        block = acc_ref[at + c * STRIP : at + (c + 1) * STRIP, :]
        out_ref[rows, c * SPAN : (c + 1) * SPAN] = block.astype(jnp.bfloat16)
    low = lax.broadcasted_iota(jnp.int32, (STRIP, LANES), 1) < 64
    out_ref[rows, span:] = jnp.where(low, after, before).astype(jnp.bfloat16)


def others_kernel(points_ref, out_ref, side_ref, first_ref, second_ref, mass_ref, acc_ref):
    quarters = out_ref.shape[0] // STRIP
    here = lax.axis_index("grp")
    share = CELLS // quarters
    sources = points_ref.shape[0] // 3
    half = sources // 2
    origin = (here + 1) * share - STRIP

    def split(ids):
        ids = ids.astype(jnp.int32)
        first = ((ids >> 8) - origin) & (CELLS - 1)
        return (first - 256).astype(jnp.float32), (ids & 255).astype(jnp.float32)

    ids = points_ref[pl.ds(0, sources, stride=3), :]
    mixed = points_ref[pl.ds(1, sources, stride=3), :]
    masses = points_ref[pl.ds(2, sources, stride=3), :]
    low = lax.broadcasted_iota(jnp.int32, (half, LANES), 1) < 64
    refs = (first_ref, second_ref, mass_ref)
    heads = [jnp.where(low, value[:half], pltpu.roll(value[half:], 64, 1)) for value in (ids, masses)]
    for ref, value in zip(refs, (*split(heads[0]), heads[1])):
        ref[:half, :] = value
    low = lax.broadcasted_iota(jnp.int32, (sources, LANES), 1) < 64
    live = jnp.concatenate(
        [
            jnp.max(jnp.where(low | (value == 0.0), 0.0, 1.0), axis=1, keepdims=True)
            for value in (masses, mixed)
        ],
        axis=0,
    )
    tails = packed_units(
        (
            [(value, True) for value in (*split(ids), masses)],
            [(value, False) for value in split(mixed)] + [(mixed, True)],
        ),
        live,
    )
    for i, ref in enumerate(refs):
        ref[half:, :] = tails[:, i * LANES : (i + 1) * LANES]
    rows = half + ((jnp.sum(live).astype(jnp.int32) + 1) >> 1)
    cells = acc_ref.shape[0]
    acc_ref[...] = one_hot_sum(cells, *refs, 0, ROWS)

    def more(i, carry):
        start = pl.multiple_of(ROWS + i * STEP, STEP)
        acc_ref[...] += one_hot_sum(cells, *refs, start, STEP)
        return carry

    lax.fori_loop(0, (jnp.maximum(rows - ROWS, 0) + STEP - 1) // STEP, more, 0)
    blank = jnp.zeros((STRIP, LANES), jnp.float32)
    for r in range(1, quarters):
        quarter = (here + r) & (quarters - 1)
        at = STRIP + (r - 1) * share
        before = jnp.where(quarter == 0, blank, acc_ref[at - STRIP : at, LANES:])
        after = jnp.where(quarter == quarters - 1, blank, acc_ref[at + share : at + share + STRIP, :LANES])
        rows = pl.ds(pl.multiple_of(quarter * STRIP, STRIP), STRIP)
        store_strip(out_ref, rows, acc_ref, at, before, after)
    out_ref[pl.ds(pl.multiple_of(here * STRIP, STRIP), STRIP), :] = jnp.zeros(
        (STRIP, out_ref.shape[1]), jnp.bfloat16
    )
    last = STRIP + (quarters - 1) * share
    side_ref[:STRIP, :] = jnp.where(here == 0, blank, acc_ref[last - STRIP : last, LANES:])
    side_ref[STRIP:, :] = jnp.where(here == quarters - 1, blank, acc_ref[STRIP : 2 * STRIP, :LANES])


def own_kernel(first_ref, second_ref, mass_ref, side_ref, out_ref, moved_ref, acc_ref):
    moved = first_ref[...] + float(out_ref.shape[1] // SPAN * STRIP - STRIP)
    moved_ref[...] = jnp.where(moved < CELLS // 2, moved, moved - CELLS)
    cells = acc_ref.shape[0]
    acc_ref[...] = one_hot_sum(cells, moved_ref, second_ref, mass_ref, 0, ROWS)
    rest = first_ref.shape[0] - ROWS

    @pl.when(jnp.max(jnp.abs(mass_ref[ROWS:, :])) > 0.0)
    def _():
        acc_ref[...] += one_hot_sum(cells, moved_ref, second_ref, mass_ref, ROWS, rest)

    before = side_ref[:STRIP, :]
    after = side_ref[STRIP:, :]
    store_strip(out_ref, pl.ds(0, STRIP), acc_ref, 0, before, after)


def band_kernel(parity_ref, kernel_ref, band_ref, odd_ref):
    parity = parity_ref[0]
    row = lax.broadcasted_iota(jnp.int32, (STRIP, 3 * TERM), 0)
    lane = lax.broadcasted_iota(jnp.int32, (STRIP, 3 * TERM), 1)
    source = lane % TERM
    near = source - PARTS
    far = near - HALO
    near = near + (1 - parity) * (STRIP + HALO)
    far = far + parity * (STRIP + HALO)
    framed = jnp.where(
        source < PARTS,
        HALO + source % STRIP,
        jnp.where(source < PARTS + HALO, near, far),
    )
    tap = framed - row
    for b in range(TAPS):
        whole = jnp.zeros(tap.shape, jnp.float32)
        for a in range(TAPS):
            whole = jnp.where(tap == a, kernel_ref[a, b], whole)
        high = whole.astype(jnp.bfloat16).astype(jnp.float32)
        rest = whole - high
        middle = rest.astype(jnp.bfloat16).astype(jnp.float32)
        term = jnp.where(lane < TERM, high, jnp.where(lane < 2 * TERM, middle, rest - middle))
        band_ref[pl.ds(b * STRIP, STRIP), :] = term
    odd_ref[...] = jnp.broadcast_to(parity.astype(jnp.float32), odd_ref.shape)


def edge_kernel(odd_ref, parts_ref, own_ref, edge_ref, *, top_if_odd):
    is_top = (odd_ref[:HALO, :] > 0.5) == top_if_odd
    for t in range(parts_ref.shape[1] // LANES):
        here = slice(t * LANES, (t + 1) * LANES)
        total = own_ref[:, here].astype(jnp.float32)
        for g in range(parts_ref.shape[0] // STRIP):
            total = total + parts_ref[g * STRIP : (g + 1) * STRIP, here].astype(jnp.float32)
        edge_ref[:, here] = jnp.where(is_top, total[:HALO], total[HALO:]).astype(jnp.bfloat16)


def smooth_kernel(band_ref, parts_ref, own_ref, near_ref, far_ref, out_ref):
    width = parts_ref.shape[1]
    near = near_ref[...].astype(jnp.float32)
    far = far_ref[...].astype(jnp.float32)
    rest = jnp.concatenate([own_ref[...].astype(jnp.float32), near, far], axis=0)
    frame = jnp.concatenate([parts_ref[...], rest.astype(jnp.bfloat16)], axis=0)
    frame = jnp.concatenate([frame, frame, frame], axis=0)
    shifted = jnp.dot(band_ref[...].astype(jnp.bfloat16), frame, preferred_element_type=jnp.float32)
    total = shifted[HALO * STRIP : (HALO + 1) * STRIP]
    for b in range(TAPS):
        if b != HALO:
            part = shifted[b * STRIP : (b + 1) * STRIP]
            total = total + pltpu.roll(part, (HALO - b) % width, 1)
    out_ref[...] = total[:, : out_ref.shape[1]]


def per_device(tile_row, pixel_col, weight, counts, kernel):
    owners = lax.axis_size("own")
    groups = lax.axis_size("grp")
    points = tile_row.shape[2] // LANES
    quarter = W // groups
    width = quarter + LANES
    packed = pl.pallas_call(
        pack_kernel,
        out_shape=jax.ShapeDtypeStruct((3 * owners, LANES), jnp.float32),
        in_specs=[pl.BlockSpec(memory_space=pltpu.HBM)] * 4,
        out_specs=vmem_spec(),
        scratch_shapes=[
            pltpu.VMEM((points, LANES), jnp.int32),
            pltpu.VMEM((points, LANES), jnp.int32),
            pltpu.VMEM((points, 1, LANES), jnp.bfloat16),
            pltpu.VMEM((1, owners), jnp.int32),
            pltpu.VMEM((points, LANES), jnp.float32),
            pltpu.SemaphoreType.DMA((4,)),
        ],
        compiler_params=limit(4),
        name="pack",
    )(
        *(
            pltpu.with_memory_space_constraint(value.reshape(shape), pltpu.HBM)
            for value, shape in (
                (tile_row, (points, LANES)),
                (pixel_col, (points, LANES)),
                (weight, (points, 1, LANES)),
                (counts, (1, owners)),
            )
        )
    )
    arrived = lax.all_to_all(
        packed.reshape(3 * owners, 1, LANES), "own", split_axis=0, concat_axis=0, tiled=True
    ).reshape(3 * owners, LANES)
    plane = jax.ShapeDtypeStruct((points, LANES), jnp.float32)
    sent, side, first, second, mass = pl.pallas_call(
        others_kernel,
        out_shape=(
            jax.ShapeDtypeStruct((groups * STRIP, width), jnp.bfloat16),
            jax.ShapeDtypeStruct((2 * STRIP, LANES), jnp.float32),
            plane,
            plane,
            plane,
        ),
        in_specs=[vmem_spec()],
        out_specs=(vmem_spec(),) * 5,
        scratch_shapes=[pltpu.VMEM((CELLS - CELLS // groups + 2 * STRIP, SPAN), jnp.float32)],
        compiler_params=limit(32),
        name="others",
    )(arrived)
    sent, kernel = lax.optimization_barrier((sent, kernel))
    parts = lax.all_to_all(sent, "grp", split_axis=0, concat_axis=0, tiled=True)
    own = pl.pallas_call(
        own_kernel,
        out_shape=jax.ShapeDtypeStruct((STRIP, width), jnp.bfloat16),
        in_specs=[vmem_spec()] * 4,
        out_specs=vmem_spec(),
        scratch_shapes=[
            pltpu.VMEM((points, LANES), jnp.float32),
            pltpu.VMEM((max(CELLS // groups, 256), SPAN), jnp.float32),
        ],
        compiler_params=limit(32),
        cost_estimate=pl.CostEstimate(flops=2 * points * LANES * W * STRIP // groups, bytes_accessed=2**19, transcendentals=0),
        name="own",
    )(first, second, mass, side)
    parity = (lax.axis_index("own") & 1).reshape(1).astype(jnp.int32)
    band, odd = pl.pallas_call(
        band_kernel,
        out_shape=(
            jax.ShapeDtypeStruct((TAPS * STRIP, 3 * TERM), jnp.float32),
            jax.ShapeDtypeStruct((STRIP, LANES), jnp.float32),
        ),
        in_specs=[smem_spec(), smem_spec()],
        out_specs=(vmem_spec(),) * 2,
        compiler_params=limit(4),
        name="band",
    )(parity, kernel)
    def edge(parts, top_if_odd, name):
        return pl.pallas_call(
            functools.partial(edge_kernel, top_if_odd=top_if_odd),
            out_shape=jax.ShapeDtypeStruct((HALO, width), jnp.bfloat16),
            in_specs=[vmem_spec()] * 3,
            out_specs=vmem_spec(),
            compiler_params=limit(4),
            name=name,
        )(odd, parts, own)

    near = edge(parts, True, "near")
    near, later = lax.optimization_barrier((near, parts))
    far = edge(later, False, "far")
    on_chip = [(i, i ^ 1) for i in range(owners)]
    across = [(i, i + 1) for i in range(1, owners - 1, 2)]
    across = across + [(j, i) for i, j in across]
    far = lax.ppermute(far, "own", across)
    near = lax.ppermute(near, "own", on_chip)
    return pl.pallas_call(
        smooth_kernel,
        out_shape=jax.ShapeDtypeStruct((STRIP, quarter), jnp.float32),
        in_specs=[vmem_spec()] * 5,
        out_specs=vmem_spec(),
        compiler_params=limit(16),
        name="smooth",
    )(band, parts, own, near, far)


def solution(mesh):
    placed = (
        P("grp", "own", None),
        P("grp", "own", None),
        P("grp", "own", None),
        P("grp", "own", None),
        P(),
    )
    return jax.shard_map(
        per_device, mesh=mesh, in_specs=placed, out_specs=P("own", "grp"), check_vma=False
    )
```

```python
import functools

import jax
import jax.numpy as jnp
from jax import lax
from jax.experimental import pallas as pl
from jax.experimental.pallas import tpu as pltpu
from jax.sharding import PartitionSpec as P

W = 16384
STRIP = 8
CAP = 192
LANES = 128
HALO = 4
TAPS = 2 * HALO + 1
PARTS = 40
TERM = 48
SPAN = 256
CELLS = STRIP * W // SPAN
ROWS = 136
STEP = 8


def vmem_spec():
    return pl.BlockSpec(memory_space=pltpu.VMEM)


def smem_spec():
    return pl.BlockSpec(memory_space=pltpu.SMEM)


def limit(mebibytes):
    return pltpu.CompilerParams(vmem_limit_bytes=mebibytes * 2**20)


def pack_kernel(row_in, col_in, weight_in, count_in, out_ref, row_ref, col_ref, weight_ref, count_ref, wide_ref, sems):
    copies = [
        pltpu.make_async_copy(source, target, sems.at[i])
        for i, (source, target) in enumerate(
            ((weight_in, weight_ref), (count_in, count_ref), (row_in, row_ref), (col_in, col_ref))
        )
    ]
    for copy in copies:
        copy.start()
    for copy in copies:
        copy.wait()
    points = row_ref.shape[0]
    pairs = points // 3
    for i in range(points):
        wide_ref[pl.ds(i, 1), :] = weight_ref[i].astype(jnp.float32)
    lane = lax.broadcasted_iota(jnp.int32, (pairs, LANES), 1)
    block = lax.broadcasted_iota(jnp.int32, (pairs, LANES), 0)
    counts = jnp.broadcast_to(count_ref[...], (pairs, LANES))
    even = jnp.sum(jnp.where(lane == 2 * block, counts, 0), axis=1, keepdims=True)
    odd = jnp.sum(jnp.where(lane == 2 * block + 1, counts, 0), axis=1, keepdims=True)
    low = lane < 64
    lives = (
        lane < even,
        jnp.where(low, lane + 128, lane - 64) < jnp.where(low, even, odd),
        lane + 64 < odd,
    )
    ids, masses = [], []
    for k in range(3):
        tile_row = row_ref[pl.ds(k, pairs, stride=3), :]
        column = col_ref[pl.ds(k, pairs, stride=3), :]
        index = (((column >> 8) * STRIP + tile_row) << 8) + (column & 255)
        ids.append(index.astype(jnp.float32))
        masses.append(jnp.where(lives[k], wide_ref[pl.ds(k, pairs, stride=3), :], 0.0))
    half = LANES // 2
    out_ref[pl.ds(0, pairs, stride=6), :] = ids[0]
    out_ref[pl.ds(1, pairs, stride=6), :] = jnp.where(low, ids[1], pltpu.roll(masses[1], half, 1))
    out_ref[pl.ds(2, pairs, stride=6), :] = masses[0]
    out_ref[pl.ds(3, pairs, stride=6), :] = pltpu.roll(jnp.where(low, ids[2], ids[1]), half, 1)
    out_ref[pl.ds(4, pairs, stride=6), :] = jnp.where(low, pltpu.roll(ids[2], half, 1), masses[2])
    out_ref[pl.ds(5, pairs, stride=6), :] = pltpu.roll(jnp.where(low, masses[2], masses[1]), half, 1)


def one_hot_sum(cells, first_ref, second_ref, mass_ref, start, rows):
    first_iota = (
        lax.broadcasted_iota(jnp.int32, (cells, LANES), 0).astype(jnp.float32) - 256.0
    ).astype(jnp.bfloat16)
    second_iota = lax.broadcasted_iota(jnp.int32, (SPAN, LANES), 0).astype(jnp.float32).astype(jnp.bfloat16)
    one = jnp.ones((), jnp.bfloat16)
    zero = jnp.zeros((), jnp.bfloat16)
    here = pl.ds(start, rows)
    first = first_ref[here, :].astype(jnp.bfloat16)
    second = second_ref[here, :].astype(jnp.bfloat16)
    mass = mass_ref[here, :].astype(jnp.bfloat16)
    left, right = [], []
    for r in range(rows):
        left.append(jnp.where(first_iota == first[r : r + 1], one, zero))
        right.append(jnp.where(second_iota == second[r : r + 1], mass[r : r + 1], zero))
    return lax.dot_general(
        jnp.concatenate(left, axis=1),
        jnp.concatenate(right, axis=1),
        (((1,), (1,)), ((), ())),
        preferred_element_type=jnp.float32,
    )


def packed_units(planes, live):
    units = live.shape[0]
    count = units // 2
    low = lax.broadcasted_iota(jnp.int32, (count, LANES), 1) < 64

    def placed(value, is_high, to_high):
        moved = value if is_high == to_high else pltpu.roll(value, 64, 1)
        return jnp.where(low, 0.0, moved) if to_high else jnp.where(low, moved, 0.0)

    sources = jnp.concatenate(
        [
            jnp.concatenate([placed(value, is_high, to_high) for value, is_high in kind], axis=1)
            for to_high in (False, True)
            for kind in planes
        ],
        axis=0,
    ).astype(jnp.bfloat16)
    row = lax.broadcasted_iota(jnp.int32, (units, units), 0)
    column = lax.broadcasted_iota(jnp.int32, (units, units), 1)
    counted = jnp.where(row < column, 1.0, jnp.where(row == column, 512.0, 0.0))
    counted = (jnp.broadcast_to(live, (units, units)) * counted).astype(jnp.bfloat16)
    place = jnp.dot(jnp.ones((8, units), jnp.bfloat16), counted, preferred_element_type=jnp.float32)
    place = jnp.broadcast_to(place[:1] - 512.0, (count, units))
    target = lax.broadcasted_iota(jnp.int32, (count, units), 0).astype(jnp.float32) * 2.0
    chosen = jnp.concatenate(
        [jnp.where(place == target, 1.0, 0.0), jnp.where(place == target + 1.0, 1.0, 0.0)], axis=1
    ).astype(jnp.bfloat16)
    return jnp.dot(chosen, sources, preferred_element_type=jnp.float32)


def store_strip(out_ref, rows, acc_ref, at, before, after):
    span = out_ref.shape[1] - LANES
    for c in range(span // SPAN):
        block = acc_ref[at + c * STRIP : at + (c + 1) * STRIP, :]
        out_ref[rows, c * SPAN : (c + 1) * SPAN] = block.astype(jnp.bfloat16)
    low = lax.broadcasted_iota(jnp.int32, (STRIP, LANES), 1) < 64
    out_ref[rows, span:] = jnp.where(low, after, before).astype(jnp.bfloat16)


def others_kernel(points_ref, out_ref, side_ref, first_ref, second_ref, mass_ref, acc_ref):
    quarters = out_ref.shape[0] // STRIP
    here = lax.axis_index("grp")
    share = CELLS // quarters
    sources = points_ref.shape[0] // 3
    half = sources // 2
    origin = (here + 1) * share - STRIP

    def split(ids):
        ids = ids.astype(jnp.int32)
        first = ((ids >> 8) - origin) & (CELLS - 1)
        return (first - 256).astype(jnp.float32), (ids & 255).astype(jnp.float32)

    ids = points_ref[pl.ds(0, sources, stride=3), :]
    mixed = points_ref[pl.ds(1, sources, stride=3), :]
    masses = points_ref[pl.ds(2, sources, stride=3), :]
    low = lax.broadcasted_iota(jnp.int32, (half, LANES), 1) < 64
    refs = (first_ref, second_ref, mass_ref)
    heads = [jnp.where(low, value[:half], pltpu.roll(value[half:], 64, 1)) for value in (ids, masses)]
    for ref, value in zip(refs, (*split(heads[0]), heads[1])):
        ref[:half, :] = value
    low = lax.broadcasted_iota(jnp.int32, (sources, LANES), 1) < 64
    live = jnp.concatenate(
        [
            jnp.max(jnp.where(low | (value == 0.0), 0.0, 1.0), axis=1, keepdims=True)
            for value in (masses, mixed)
        ],
        axis=0,
    )
    tails = packed_units(
        (
            [(value, True) for value in (*split(ids), masses)],
            [(value, False) for value in split(mixed)] + [(mixed, True)],
        ),
        live,
    )
    for i, ref in enumerate(refs):
        ref[half:, :] = tails[:, i * LANES : (i + 1) * LANES]
    rows = half + ((jnp.sum(live).astype(jnp.int32) + 1) >> 1)
    cells = acc_ref.shape[0]
    acc_ref[...] = one_hot_sum(cells, *refs, 0, ROWS)

    def more(i, carry):
        start = pl.multiple_of(ROWS + i * STEP, STEP)
        acc_ref[...] += one_hot_sum(cells, *refs, start, STEP)
        return carry

    lax.fori_loop(0, (jnp.maximum(rows - ROWS, 0) + STEP - 1) // STEP, more, 0)
    blank = jnp.zeros((STRIP, LANES), jnp.float32)
    for r in range(1, quarters):
        quarter = (here + r) & (quarters - 1)
        at = STRIP + (r - 1) * share
        before = jnp.where(quarter == 0, blank, acc_ref[at - STRIP : at, LANES:])
        after = jnp.where(quarter == quarters - 1, blank, acc_ref[at + share : at + share + STRIP, :LANES])
        rows = pl.ds(pl.multiple_of(quarter * STRIP, STRIP), STRIP)
        store_strip(out_ref, rows, acc_ref, at, before, after)
    out_ref[pl.ds(pl.multiple_of(here * STRIP, STRIP), STRIP), :] = jnp.zeros(
        (STRIP, out_ref.shape[1]), jnp.bfloat16
    )
    last = STRIP + (quarters - 1) * share
    side_ref[:STRIP, :] = jnp.where(here == 0, blank, acc_ref[last - STRIP : last, LANES:])
    side_ref[STRIP:, :] = jnp.where(here == quarters - 1, blank, acc_ref[STRIP : 2 * STRIP, :LANES])


def own_kernel(first_ref, second_ref, mass_ref, side_ref, out_ref, moved_ref, acc_ref):
    moved = first_ref[...] + float(out_ref.shape[1] // SPAN * STRIP - STRIP)
    moved_ref[...] = jnp.where(moved < CELLS // 2, moved, moved - CELLS)
    cells = acc_ref.shape[0]
    acc_ref[...] = one_hot_sum(cells, moved_ref, second_ref, mass_ref, 0, ROWS)
    rest = first_ref.shape[0] - ROWS

    @pl.when(jnp.max(jnp.abs(mass_ref[ROWS:, :])) > 0.0)
    def _():
        acc_ref[...] += one_hot_sum(cells, moved_ref, second_ref, mass_ref, ROWS, rest)

    before = side_ref[:STRIP, :]
    after = side_ref[STRIP:, :]
    store_strip(out_ref, pl.ds(0, STRIP), acc_ref, 0, before, after)


def band_kernel(parity_ref, kernel_ref, band_ref, odd_ref):
    parity = parity_ref[0]
    row = lax.broadcasted_iota(jnp.int32, (STRIP, 3 * TERM), 0)
    lane = lax.broadcasted_iota(jnp.int32, (STRIP, 3 * TERM), 1)
    source = lane % TERM
    near = source - PARTS
    far = near - HALO
    near = near + (1 - parity) * (STRIP + HALO)
    far = far + parity * (STRIP + HALO)
    framed = jnp.where(
        source < PARTS,
        HALO + source % STRIP,
        jnp.where(source < PARTS + HALO, near, far),
    )
    tap = framed - row
    for b in range(TAPS):
        whole = jnp.zeros(tap.shape, jnp.float32)
        for a in range(TAPS):
            whole = jnp.where(tap == a, kernel_ref[a, b], whole)
        high = whole.astype(jnp.bfloat16).astype(jnp.float32)
        rest = whole - high
        middle = rest.astype(jnp.bfloat16).astype(jnp.float32)
        term = jnp.where(lane < TERM, high, jnp.where(lane < 2 * TERM, middle, rest - middle))
        band_ref[pl.ds(b * STRIP, STRIP), :] = term
    odd_ref[...] = jnp.broadcast_to(parity.astype(jnp.float32), odd_ref.shape)


def edge_kernel(odd_ref, parts_ref, own_ref, edge_ref, *, top_if_odd):
    is_top = (odd_ref[:HALO, :] > 0.5) == top_if_odd
    for t in range(parts_ref.shape[1] // LANES):
        here = slice(t * LANES, (t + 1) * LANES)
        total = own_ref[:, here].astype(jnp.float32)
        for g in range(parts_ref.shape[0] // STRIP):
            total = total + parts_ref[g * STRIP : (g + 1) * STRIP, here].astype(jnp.float32)
        edge_ref[:, here] = jnp.where(is_top, total[:HALO], total[HALO:]).astype(jnp.bfloat16)


def smooth_kernel(band_ref, parts_ref, own_ref, near_ref, far_ref, out_ref):
    width = parts_ref.shape[1]
    near = near_ref[...].astype(jnp.float32)
    far = far_ref[...].astype(jnp.float32)
    rest = jnp.concatenate([own_ref[...].astype(jnp.float32), near, far], axis=0)
    frame = jnp.concatenate([parts_ref[...], rest.astype(jnp.bfloat16)], axis=0)
    frame = jnp.concatenate([frame, frame, frame], axis=0)
    shifted = jnp.dot(band_ref[...].astype(jnp.bfloat16), frame, preferred_element_type=jnp.float32)
    total = shifted[HALO * STRIP : (HALO + 1) * STRIP]
    for b in range(TAPS):
        if b != HALO:
            part = shifted[b * STRIP : (b + 1) * STRIP]
            total = total + pltpu.roll(part, (HALO - b) % width, 1)
    out_ref[...] = total[:, : out_ref.shape[1]]


def per_device(tile_row, pixel_col, weight, counts, kernel):
    owners = lax.axis_size("own")
    groups = lax.axis_size("grp")
    points = tile_row.shape[2] // LANES
    quarter = W // groups
    width = quarter + LANES
    packed = pl.pallas_call(
        pack_kernel,
        out_shape=jax.ShapeDtypeStruct((3 * owners, LANES), jnp.float32),
        in_specs=[pl.BlockSpec(memory_space=pltpu.HBM)] * 4,
        out_specs=vmem_spec(),
        scratch_shapes=[
            pltpu.VMEM((points, LANES), jnp.int32),
            pltpu.VMEM((points, LANES), jnp.int32),
            pltpu.VMEM((points, 1, LANES), jnp.bfloat16),
            pltpu.VMEM((1, owners), jnp.int32),
            pltpu.VMEM((points, LANES), jnp.float32),
            pltpu.SemaphoreType.DMA((4,)),
        ],
        compiler_params=limit(4),
        name="pack",
    )(
        *(
            pltpu.with_memory_space_constraint(value.reshape(shape), pltpu.HBM)
            for value, shape in (
                (tile_row, (points, LANES)),
                (pixel_col, (points, LANES)),
                (weight, (points, 1, LANES)),
                (counts, (1, owners)),
            )
        )
    )
    arrived = lax.all_to_all(
        packed.reshape(3 * owners, 1, LANES), "own", split_axis=0, concat_axis=0, tiled=True
    ).reshape(3 * owners, LANES)
    plane = jax.ShapeDtypeStruct((points, LANES), jnp.float32)
    sent, side, first, second, mass = pl.pallas_call(
        others_kernel,
        out_shape=(
            jax.ShapeDtypeStruct((groups * STRIP, width), jnp.bfloat16),
            jax.ShapeDtypeStruct((2 * STRIP, LANES), jnp.float32),
            plane,
            plane,
            plane,
        ),
        in_specs=[vmem_spec()],
        out_specs=(vmem_spec(),) * 5,
        scratch_shapes=[pltpu.VMEM((CELLS - CELLS // groups + 2 * STRIP, SPAN), jnp.float32)],
        compiler_params=limit(32),
        name="others",
    )(arrived)
    sent, kernel = lax.optimization_barrier((sent, kernel))
    parts = lax.all_to_all(sent, "grp", split_axis=0, concat_axis=0, tiled=True)
    own = pl.pallas_call(
        own_kernel,
        out_shape=jax.ShapeDtypeStruct((STRIP, width), jnp.bfloat16),
        in_specs=[vmem_spec()] * 4,
        out_specs=vmem_spec(),
        scratch_shapes=[
            pltpu.VMEM((points, LANES), jnp.float32),
            pltpu.VMEM((max(CELLS // groups, 256), SPAN), jnp.float32),
        ],
        compiler_params=limit(32),
        cost_estimate=pl.CostEstimate(flops=2 * points * LANES * W * STRIP // groups, bytes_accessed=2**19, transcendentals=0),
        name="own",
    )(first, second, mass, side)
    parity = (lax.axis_index("own") & 1).reshape(1).astype(jnp.int32)
    band, odd = pl.pallas_call(
        band_kernel,
        out_shape=(
            jax.ShapeDtypeStruct((TAPS * STRIP, 3 * TERM), jnp.float32),
            jax.ShapeDtypeStruct((STRIP, LANES), jnp.float32),
        ),
        in_specs=[smem_spec(), smem_spec()],
        out_specs=(vmem_spec(),) * 2,
        compiler_params=limit(4),
        name="band",
    )(parity, kernel)
    def edge(parts, top_if_odd, name):
        return pl.pallas_call(
            functools.partial(edge_kernel, top_if_odd=top_if_odd),
            out_shape=jax.ShapeDtypeStruct((HALO, width), jnp.bfloat16),
            in_specs=[vmem_spec()] * 3,
            out_specs=vmem_spec(),
            compiler_params=limit(4),
            name=name,
        )(odd, parts, own)

    near = edge(parts, True, "near")
    near, later = lax.optimization_barrier((near, parts))
    far = edge(later, False, "far")
    on_chip = [(i, i ^ 1) for i in range(owners)]
    across = [(i, i + 1) for i in range(1, owners - 1, 2)]
    across = across + [(j, i) for i, j in across]
    far = lax.ppermute(far, "own", across)
    near = lax.ppermute(near, "own", on_chip)
    return pl.pallas_call(
        smooth_kernel,
        out_shape=jax.ShapeDtypeStruct((STRIP, quarter), jnp.float32),
        in_specs=[vmem_spec()] * 5,
        out_specs=vmem_spec(),
        compiler_params=limit(16),
        name="smooth",
    )(band, parts, own, near, far)


def solution(mesh):
    placed = (
        P("grp", "own", None),
        P("grp", "own", None),
        P("grp", "own", None),
        P("grp", "own", None),
        P(),
    )
    return jax.shard_map(
        per_device, mesh=mesh, in_specs=placed, out_specs=P("own", "grp"), check_vma=False
    )
```

```python
import functools

import jax
import jax.numpy as jnp
from jax import lax
from jax.experimental import pallas as pl
from jax.experimental.pallas import tpu as pltpu
from jax.sharding import PartitionSpec as P

W = 16384
STRIP = 8
CAP = 192
LANES = 128
HALO = 4
PLANE = 8
TAPS = 2 * HALO + 1
PARTS = 40
TERM = 48
SPAN = 256
CELLS = STRIP * W // SPAN
ROWS = 136
STEP = 8


def vmem_spec():
    return pl.BlockSpec(memory_space=pltpu.VMEM)


def smem_spec():
    return pl.BlockSpec(memory_space=pltpu.SMEM)


def limit(mebibytes):
    return pltpu.CompilerParams(vmem_limit_bytes=mebibytes * 2**20)


def ring_order(length):
    half = length // 2
    order = []
    for step in range(half):
        order += [half + step, half - 1 - step]
    return order


def pack_kernel(
    row_in, col_in, weight_in, count_in, out_ref, row_ref, col_ref, weight_ref, count_ref, wide_ref, sorted_ref, sems
):
    copies = [
        pltpu.make_async_copy(source, target, sems.at[i])
        for i, (source, target) in enumerate(
            ((weight_in, weight_ref), (count_in, count_ref), (row_in, row_ref), (col_in, col_ref))
        )
    ]
    for copy in copies:
        copy.start()
    for copy in copies:
        copy.wait()
    points = row_ref.shape[0]
    planes = out_ref.shape[0] // (3 * PLANE)
    for i in range(points):
        wide_ref[pl.ds(i, 1), :] = weight_ref[i].astype(jnp.float32)
    lane = lax.broadcasted_iota(jnp.int32, (planes, LANES), 1)
    plane = lax.broadcasted_iota(jnp.int32, (planes, LANES), 0)
    counts = jnp.broadcast_to(count_ref[...], (planes, LANES))
    low = lane < 64
    half = LANES // 2
    for y in range(PLANE // 2):
        block = plane * PLANE + 2 * y
        even = jnp.sum(jnp.where(lane == block, counts, 0), axis=1, keepdims=True)
        odd = jnp.sum(jnp.where(lane == block + 1, counts, 0), axis=1, keepdims=True)
        lives = (
            lane < even,
            jnp.where(low, lane + 128, lane - 64) < jnp.where(low, even, odd),
            lane + 64 < odd,
        )
        ids, masses = [], []
        for k in range(3):
            rows = pl.ds(3 * y + k, planes, stride=3 * PLANE // 2)
            index = (((col_ref[rows, :] >> 8) * STRIP + row_ref[rows, :]) << 8) + (col_ref[rows, :] & 255)
            ids.append(index.astype(jnp.float32))
            masses.append(jnp.where(lives[k], wide_ref[rows, :], 0.0))
        for block, rows in (
            (2 * y, (ids[0], jnp.where(low, ids[1], pltpu.roll(masses[1], half, 1)), masses[0])),
            (
                2 * y + 1,
                (
                    pltpu.roll(jnp.where(low, ids[2], ids[1]), half, 1),
                    jnp.where(low, pltpu.roll(ids[2], half, 1), masses[2]),
                    pltpu.roll(jnp.where(low, masses[2], masses[1]), half, 1),
                ),
            ),
        ):
            for r, value in enumerate(rows):
                at = 3 * (PLANE - 1 - block) + r
                sorted_ref[pl.ds(at, planes, stride=3 * PLANE), :] = value
    size = 3 * PLANE
    for place, z in enumerate(ring_order(planes)):
        out_ref[pl.ds(place * size, size), :] = sorted_ref[pl.ds(z * size, size), :]


def one_hot_sum(cells, first_ref, second_ref, mass_ref, start, rows):
    first_iota = (
        lax.broadcasted_iota(jnp.int32, (cells, LANES), 0).astype(jnp.float32) - 256.0
    ).astype(jnp.bfloat16)
    second_iota = lax.broadcasted_iota(jnp.int32, (SPAN, LANES), 0).astype(jnp.float32).astype(jnp.bfloat16)
    one = jnp.ones((), jnp.bfloat16)
    zero = jnp.zeros((), jnp.bfloat16)
    here = pl.ds(start, rows)
    first = first_ref[here, :].astype(jnp.bfloat16)
    second = second_ref[here, :].astype(jnp.bfloat16)
    mass = mass_ref[here, :].astype(jnp.bfloat16)
    left, right = [], []
    for r in range(rows):
        left.append(jnp.where(first_iota == first[r : r + 1], one, zero))
        right.append(jnp.where(second_iota == second[r : r + 1], mass[r : r + 1], zero))
    return lax.dot_general(
        jnp.concatenate(left, axis=1),
        jnp.concatenate(right, axis=1),
        (((1,), (1,)), ((), ())),
        preferred_element_type=jnp.float32,
    )


def packed_units(planes, live):
    units = live.shape[0]
    count = units // 2
    low = lax.broadcasted_iota(jnp.int32, (count, LANES), 1) < 64

    def placed(value, is_high, to_high):
        moved = value if is_high == to_high else pltpu.roll(value, 64, 1)
        return jnp.where(low, 0.0, moved) if to_high else jnp.where(low, moved, 0.0)

    sources = jnp.concatenate(
        [
            jnp.concatenate([placed(value, is_high, to_high) for value, is_high in kind], axis=1)
            for to_high in (False, True)
            for kind in planes
        ],
        axis=0,
    ).astype(jnp.bfloat16)
    row = lax.broadcasted_iota(jnp.int32, (units, units), 0)
    column = lax.broadcasted_iota(jnp.int32, (units, units), 1)
    counted = jnp.where(row < column, 1.0, jnp.where(row == column, 512.0, 0.0))
    counted = (jnp.broadcast_to(live, (units, units)) * counted).astype(jnp.bfloat16)
    place = jnp.dot(jnp.ones((8, units), jnp.bfloat16), counted, preferred_element_type=jnp.float32)
    place = jnp.broadcast_to(place[:1] - 512.0, (count, units))
    target = lax.broadcasted_iota(jnp.int32, (count, units), 0).astype(jnp.float32) * 2.0
    chosen = jnp.concatenate(
        [jnp.where(place == target, 1.0, 0.0), jnp.where(place == target + 1.0, 1.0, 0.0)], axis=1
    ).astype(jnp.bfloat16)
    return jnp.dot(chosen, sources, preferred_element_type=jnp.float32)


def store_strip(out_ref, rows, acc_ref, at, before, after):
    span = out_ref.shape[1] - LANES
    for c in range(span // SPAN):
        block = acc_ref[at + c * STRIP : at + (c + 1) * STRIP, :]
        out_ref[rows, c * SPAN : (c + 1) * SPAN] = block.astype(jnp.bfloat16)
    low = lax.broadcasted_iota(jnp.int32, (STRIP, LANES), 1) < 64
    out_ref[rows, span:] = jnp.where(low, after, before).astype(jnp.bfloat16)


def others_kernel(points_ref, out_ref, side_ref, first_ref, second_ref, mass_ref, acc_ref):
    quarters = out_ref.shape[0] // STRIP
    here = lax.axis_index("grp")
    share = CELLS // quarters
    sources = points_ref.shape[0] // 3
    half = sources // 2
    origin = (here + 1) * share - STRIP

    def split(ids):
        ids = ids.astype(jnp.int32)
        first = ((ids >> 8) - origin) & (CELLS - 1)
        return (first - 256).astype(jnp.float32), (ids & 255).astype(jnp.float32)

    ids = points_ref[pl.ds(0, sources, stride=3), :]
    mixed = points_ref[pl.ds(1, sources, stride=3), :]
    masses = points_ref[pl.ds(2, sources, stride=3), :]
    low = lax.broadcasted_iota(jnp.int32, (half, LANES), 1) < 64
    refs = (first_ref, second_ref, mass_ref)
    heads = [jnp.where(low, value[:half], pltpu.roll(value[half:], 64, 1)) for value in (ids, masses)]
    for ref, value in zip(refs, (*split(heads[0]), heads[1])):
        ref[:half, :] = value
    low = lax.broadcasted_iota(jnp.int32, (sources, LANES), 1) < 64
    live = jnp.concatenate(
        [
            jnp.max(jnp.where(low | (value == 0.0), 0.0, 1.0), axis=1, keepdims=True)
            for value in (masses, mixed)
        ],
        axis=0,
    )
    tails = packed_units(
        (
            [(value, True) for value in (*split(ids), masses)],
            [(value, False) for value in split(mixed)] + [(mixed, True)],
        ),
        live,
    )
    for i, ref in enumerate(refs):
        ref[half:, :] = tails[:, i * LANES : (i + 1) * LANES]
    rows = half + ((jnp.sum(live).astype(jnp.int32) + 1) >> 1)
    cells = acc_ref.shape[0]
    acc_ref[...] = one_hot_sum(cells, *refs, 0, ROWS)

    def more(i, carry):
        start = pl.multiple_of(ROWS + i * STEP, STEP)
        acc_ref[...] += one_hot_sum(cells, *refs, start, STEP)
        return carry

    lax.fori_loop(0, (jnp.maximum(rows - ROWS, 0) + STEP - 1) // STEP, more, 0)
    blank = jnp.zeros((STRIP, LANES), jnp.float32)
    for r in range(1, quarters):
        quarter = (here + r) & (quarters - 1)
        at = STRIP + (r - 1) * share
        before = jnp.where(quarter == 0, blank, acc_ref[at - STRIP : at, LANES:])
        after = jnp.where(quarter == quarters - 1, blank, acc_ref[at + share : at + share + STRIP, :LANES])
        rows = pl.ds(pl.multiple_of(quarter * STRIP, STRIP), STRIP)
        store_strip(out_ref, rows, acc_ref, at, before, after)
    out_ref[pl.ds(pl.multiple_of(here * STRIP, STRIP), STRIP), :] = jnp.zeros(
        (STRIP, out_ref.shape[1]), jnp.bfloat16
    )
    last = STRIP + (quarters - 1) * share
    side_ref[:STRIP, :] = jnp.where(here == 0, blank, acc_ref[last - STRIP : last, LANES:])
    side_ref[STRIP:, :] = jnp.where(here == quarters - 1, blank, acc_ref[STRIP : 2 * STRIP, :LANES])


def own_kernel(first_ref, second_ref, mass_ref, side_ref, out_ref, moved_ref, acc_ref):
    moved = first_ref[...] + float(out_ref.shape[1] // SPAN * STRIP - STRIP)
    moved_ref[...] = jnp.where(moved < CELLS // 2, moved, moved - CELLS)
    cells = acc_ref.shape[0]
    acc_ref[...] = one_hot_sum(cells, moved_ref, second_ref, mass_ref, 0, ROWS)
    rest = first_ref.shape[0] - ROWS

    @pl.when(jnp.max(jnp.abs(mass_ref[ROWS:, :])) > 0.0)
    def _():
        acc_ref[...] += one_hot_sum(cells, moved_ref, second_ref, mass_ref, ROWS, rest)

    before = side_ref[:STRIP, :]
    after = side_ref[STRIP:, :]
    store_strip(out_ref, pl.ds(0, STRIP), acc_ref, 0, before, after)


def band_kernel(parity_ref, kernel_ref, band_ref, odd_ref):
    parity = parity_ref[0]
    row = lax.broadcasted_iota(jnp.int32, (STRIP, 3 * TERM), 0)
    lane = lax.broadcasted_iota(jnp.int32, (STRIP, 3 * TERM), 1)
    source = lane % TERM
    near = source - PARTS
    far = near - HALO
    near = near + (1 - parity) * (STRIP + HALO)
    far = far + parity * (STRIP + HALO)
    framed = jnp.where(
        source < PARTS,
        HALO + source % STRIP,
        jnp.where(source < PARTS + HALO, near, far),
    )
    tap = framed - row
    for b in range(TAPS):
        whole = jnp.zeros(tap.shape, jnp.float32)
        for a in range(TAPS):
            whole = jnp.where(tap == a, kernel_ref[a, b], whole)
        high = whole.astype(jnp.bfloat16).astype(jnp.float32)
        rest = whole - high
        middle = rest.astype(jnp.bfloat16).astype(jnp.float32)
        term = jnp.where(lane < TERM, high, jnp.where(lane < 2 * TERM, middle, rest - middle))
        band_ref[pl.ds(b * STRIP, STRIP), :] = term
    odd_ref[...] = jnp.broadcast_to(parity.astype(jnp.float32), odd_ref.shape)


def edge_kernel(odd_ref, parts_ref, own_ref, edge_ref, *, top_if_odd):
    is_top = (odd_ref[:HALO, :] > 0.5) == top_if_odd
    for t in range(parts_ref.shape[1] // LANES):
        here = slice(t * LANES, (t + 1) * LANES)
        total = own_ref[:, here].astype(jnp.float32)
        for g in range(parts_ref.shape[0] // STRIP):
            total = total + parts_ref[g * STRIP : (g + 1) * STRIP, here].astype(jnp.float32)
        edge_ref[:, here] = jnp.where(is_top, total[:HALO], total[HALO:]).astype(jnp.bfloat16)


def smooth_kernel(band_ref, parts_ref, own_ref, near_ref, far_ref, out_ref):
    width = parts_ref.shape[1]
    near = near_ref[...].astype(jnp.float32)
    far = far_ref[...].astype(jnp.float32)
    rest = jnp.concatenate([own_ref[...].astype(jnp.float32), near, far], axis=0)
    frame = jnp.concatenate([parts_ref[...], rest.astype(jnp.bfloat16)], axis=0)
    frame = jnp.concatenate([frame, frame, frame], axis=0)
    shifted = jnp.dot(band_ref[...].astype(jnp.bfloat16), frame, preferred_element_type=jnp.float32)
    total = shifted[HALO * STRIP : (HALO + 1) * STRIP]
    for b in range(TAPS):
        if b != HALO:
            part = shifted[b * STRIP : (b + 1) * STRIP]
            total = total + pltpu.roll(part, (HALO - b) % width, 1)
    out_ref[...] = total[:, : out_ref.shape[1]]


def per_device(tile_row, pixel_col, weight, counts, kernel):
    owners = lax.axis_size("own")
    groups = lax.axis_size("grp")
    points = tile_row.shape[2] // LANES
    quarter = W // groups
    width = quarter + LANES
    packed = pl.pallas_call(
        pack_kernel,
        out_shape=jax.ShapeDtypeStruct((3 * owners, LANES), jnp.float32),
        in_specs=[pl.BlockSpec(memory_space=pltpu.HBM)] * 4,
        out_specs=vmem_spec(),
        scratch_shapes=[
            pltpu.VMEM((points, LANES), jnp.int32),
            pltpu.VMEM((points, LANES), jnp.int32),
            pltpu.VMEM((points, 1, LANES), jnp.bfloat16),
            pltpu.VMEM((1, owners), jnp.int32),
            pltpu.VMEM((points, LANES), jnp.float32),
            pltpu.VMEM((3 * owners, LANES), jnp.float32),
            pltpu.SemaphoreType.DMA((4,)),
        ],
        compiler_params=limit(4),
        name="pack",
    )(
        *(
            pltpu.with_memory_space_constraint(value.reshape(shape), pltpu.HBM)
            for value, shape in (
                (tile_row, (points, LANES)),
                (pixel_col, (points, LANES)),
                (weight, (points, 1, LANES)),
                (counts, (1, owners)),
            )
        )
    )
    order = [z * PLANE + k for z in ring_order(owners // PLANE) for k in reversed(range(PLANE))]
    arrived = lax.all_to_all(
        packed.reshape(3 * owners, 1, LANES),
        "own",
        split_axis=0,
        concat_axis=0,
        tiled=True,
        axis_index_groups=[order],
    ).reshape(3 * owners, LANES)
    plane = jax.ShapeDtypeStruct((points, LANES), jnp.float32)
    sent, side, first, second, mass = pl.pallas_call(
        others_kernel,
        out_shape=(
            jax.ShapeDtypeStruct((groups * STRIP, width), jnp.bfloat16),
            jax.ShapeDtypeStruct((2 * STRIP, LANES), jnp.float32),
            plane,
            plane,
            plane,
        ),
        in_specs=[vmem_spec()],
        out_specs=(vmem_spec(),) * 5,
        scratch_shapes=[pltpu.VMEM((CELLS - CELLS // groups + 2 * STRIP, SPAN), jnp.float32)],
        compiler_params=limit(32),
        name="others",
    )(arrived)
    sent, kernel = lax.optimization_barrier((sent, kernel))
    parts = lax.all_to_all(sent, "grp", split_axis=0, concat_axis=0, tiled=True)
    own = pl.pallas_call(
        own_kernel,
        out_shape=jax.ShapeDtypeStruct((STRIP, width), jnp.bfloat16),
        in_specs=[vmem_spec()] * 4,
        out_specs=vmem_spec(),
        scratch_shapes=[
            pltpu.VMEM((points, LANES), jnp.float32),
            pltpu.VMEM((max(CELLS // groups, 256), SPAN), jnp.float32),
        ],
        compiler_params=limit(32),
        cost_estimate=pl.CostEstimate(flops=2 * points * LANES * W * STRIP // groups, bytes_accessed=2**19, transcendentals=0),
        name="own",
    )(first, second, mass, side)
    parity = (lax.axis_index("own") & 1).reshape(1).astype(jnp.int32)
    band, odd = pl.pallas_call(
        band_kernel,
        out_shape=(
            jax.ShapeDtypeStruct((TAPS * STRIP, 3 * TERM), jnp.float32),
            jax.ShapeDtypeStruct((STRIP, LANES), jnp.float32),
        ),
        in_specs=[smem_spec(), smem_spec()],
        out_specs=(vmem_spec(),) * 2,
        compiler_params=limit(4),
        name="band",
    )(parity, kernel)
    def edge(parts, top_if_odd, name):
        return pl.pallas_call(
            functools.partial(edge_kernel, top_if_odd=top_if_odd),
            out_shape=jax.ShapeDtypeStruct((HALO, width), jnp.bfloat16),
            in_specs=[vmem_spec()] * 3,
            out_specs=vmem_spec(),
            compiler_params=limit(4),
            name=name,
        )(odd, parts, own)

    near = edge(parts, True, "near")
    near, later = lax.optimization_barrier((near, parts))
    far = edge(later, False, "far")
    on_chip = [(i, i ^ 1) for i in range(owners)]
    across = [(i, i + 1) for i in range(1, owners - 1, 2)]
    across = across + [(j, i) for i, j in across]
    far = lax.ppermute(far, "own", across)
    near = lax.ppermute(near, "own", on_chip)
    return pl.pallas_call(
        smooth_kernel,
        out_shape=jax.ShapeDtypeStruct((STRIP, quarter), jnp.float32),
        in_specs=[vmem_spec()] * 5,
        out_specs=vmem_spec(),
        compiler_params=limit(16),
        name="smooth",
    )(band, parts, own, near, far)


def solution(mesh):
    placed = (
        P("grp", "own", None),
        P("grp", "own", None),
        P("grp", "own", None),
        P("grp", "own", None),
        P(),
    )
    return jax.shard_map(
        per_device, mesh=mesh, in_specs=placed, out_specs=P("own", "grp"), check_vma=False
    )
```

```python
import functools

import jax
import jax.numpy as jnp
from jax import lax
from jax.experimental import pallas as pl
from jax.experimental.pallas import tpu as pltpu
from jax.sharding import PartitionSpec as P

W = 16384
STRIP = 8
CAP = 192
LANES = 128
HALO = 4
PLANE = 8
TAPS = 2 * HALO + 1
PARTS = 40
TERM = 48
SPAN = 256
CELLS = STRIP * W // SPAN
ROWS = 136
STEP = 8


def vmem_spec():
    return pl.BlockSpec(memory_space=pltpu.VMEM)


def smem_spec():
    return pl.BlockSpec(memory_space=pltpu.SMEM)


def limit(mebibytes):
    return pltpu.CompilerParams(vmem_limit_bytes=mebibytes * 2**20)


def ring_order(length):
    half = length // 2
    order = []
    for step in range(half):
        order += [half + step, half - 1 - step]
    return order


def pack_kernel(
    row_in, col_in, weight_in, count_in, out_ref, row_ref, col_ref, weight_ref, count_ref, wide_ref, sorted_ref, sems
):
    copies = [
        pltpu.make_async_copy(source, target, sems.at[i])
        for i, (source, target) in enumerate(
            ((weight_in, weight_ref), (count_in, count_ref), (row_in, row_ref), (col_in, col_ref))
        )
    ]
    for copy in copies:
        copy.start()
    for copy in copies:
        copy.wait()
    points = row_ref.shape[0]
    planes = out_ref.shape[0] // (3 * PLANE)
    for i in range(points):
        wide_ref[pl.ds(i, 1), :] = weight_ref[i].astype(jnp.float32)
    lane = lax.broadcasted_iota(jnp.int32, (planes, LANES), 1)
    plane = lax.broadcasted_iota(jnp.int32, (planes, LANES), 0)
    counts = jnp.broadcast_to(count_ref[...], (planes, LANES))
    low = lane < 64
    half = LANES // 2
    for y in range(PLANE // 2):
        block = plane * PLANE + 2 * y
        even = jnp.sum(jnp.where(lane == block, counts, 0), axis=1, keepdims=True)
        odd = jnp.sum(jnp.where(lane == block + 1, counts, 0), axis=1, keepdims=True)
        lives = (
            lane < even,
            jnp.where(low, lane + 128, lane - 64) < jnp.where(low, even, odd),
            lane + 64 < odd,
        )
        ids, masses = [], []
        for k in range(3):
            rows = pl.ds(3 * y + k, planes, stride=3 * PLANE // 2)
            index = (((col_ref[rows, :] >> 8) * STRIP + row_ref[rows, :]) << 8) + (col_ref[rows, :] & 255)
            ids.append(index.astype(jnp.float32))
            masses.append(jnp.where(lives[k], wide_ref[rows, :], 0.0))
        for block, rows in (
            (2 * y, (ids[0], jnp.where(low, ids[1], pltpu.roll(masses[1], half, 1)), masses[0])),
            (
                2 * y + 1,
                (
                    pltpu.roll(jnp.where(low, ids[2], ids[1]), half, 1),
                    jnp.where(low, pltpu.roll(ids[2], half, 1), masses[2]),
                    pltpu.roll(jnp.where(low, masses[2], masses[1]), half, 1),
                ),
            ),
        ):
            for r, value in enumerate(rows):
                at = 3 * (PLANE - 1 - block) + r
                sorted_ref[pl.ds(at, planes, stride=3 * PLANE), :] = value
    size = 3 * PLANE
    for place, z in enumerate(ring_order(planes)):
        out_ref[pl.ds(place * size, size), :] = sorted_ref[pl.ds(z * size, size), :]


def one_hot_sum(cells, first_ref, second_ref, mass_ref, start, rows):
    first_iota = (
        lax.broadcasted_iota(jnp.int32, (cells, LANES), 0).astype(jnp.float32) - 256.0
    ).astype(jnp.bfloat16)
    second_iota = lax.broadcasted_iota(jnp.int32, (SPAN, LANES), 0).astype(jnp.float32).astype(jnp.bfloat16)
    one = jnp.ones((), jnp.bfloat16)
    zero = jnp.zeros((), jnp.bfloat16)
    here = pl.ds(start, rows)
    first = first_ref[here, :].astype(jnp.bfloat16)
    second = second_ref[here, :].astype(jnp.bfloat16)
    mass = mass_ref[here, :].astype(jnp.bfloat16)
    left, right = [], []
    for r in range(rows):
        left.append(jnp.where(first_iota == first[r : r + 1], one, zero))
        right.append(jnp.where(second_iota == second[r : r + 1], mass[r : r + 1], zero))
    return lax.dot_general(
        jnp.concatenate(left, axis=1),
        jnp.concatenate(right, axis=1),
        (((1,), (1,)), ((), ())),
        preferred_element_type=jnp.float32,
    )


def packed_units(planes, live):
    units = live.shape[0]
    count = units // 2
    low = lax.broadcasted_iota(jnp.int32, (count, LANES), 1) < 64

    def placed(value, is_high, to_high):
        moved = value if is_high == to_high else pltpu.roll(value, 64, 1)
        return jnp.where(low, 0.0, moved) if to_high else jnp.where(low, moved, 0.0)

    sources = jnp.concatenate(
        [
            jnp.concatenate([placed(value, is_high, to_high) for value, is_high in kind], axis=1)
            for to_high in (False, True)
            for kind in planes
        ],
        axis=0,
    ).astype(jnp.bfloat16)
    row = lax.broadcasted_iota(jnp.int32, (units, units), 0)
    column = lax.broadcasted_iota(jnp.int32, (units, units), 1)
    counted = jnp.where(row < column, 1.0, jnp.where(row == column, 512.0, 0.0))
    counted = (jnp.broadcast_to(live, (units, units)) * counted).astype(jnp.bfloat16)
    place = jnp.dot(jnp.ones((8, units), jnp.bfloat16), counted, preferred_element_type=jnp.float32)
    place = jnp.broadcast_to(place[:1] - 512.0, (count, units))
    target = lax.broadcasted_iota(jnp.int32, (count, units), 0).astype(jnp.float32) * 2.0
    chosen = jnp.concatenate(
        [jnp.where(place == target, 1.0, 0.0), jnp.where(place == target + 1.0, 1.0, 0.0)], axis=1
    ).astype(jnp.bfloat16)
    return jnp.dot(chosen, sources, preferred_element_type=jnp.float32)


def store_strip(out_ref, rows, acc_ref, at, before, after):
    span = out_ref.shape[1] - LANES
    for c in range(span // SPAN):
        block = acc_ref[at + c * STRIP : at + (c + 1) * STRIP, :]
        out_ref[rows, c * SPAN : (c + 1) * SPAN] = block.astype(jnp.bfloat16)
    low = lax.broadcasted_iota(jnp.int32, (STRIP, LANES), 1) < 64
    out_ref[rows, span:] = jnp.where(low, after, before).astype(jnp.bfloat16)


def others_kernel(points_ref, out_ref, side_ref, first_ref, second_ref, mass_ref, acc_ref):
    quarters = out_ref.shape[0] // STRIP
    here = lax.axis_index("grp")
    share = CELLS // quarters
    sources = points_ref.shape[0] // 3
    half = sources // 2
    origin = (here + 1) * share - STRIP

    def place_of(quarter):
        return sum(jnp.where(quarter == q, place, 0) for place, q in enumerate(ring_order(quarters)))

    def split(ids):
        ids = ids.astype(jnp.int32)
        first = ((ids >> 8) - origin) & (CELLS - 1)
        return (first - 256).astype(jnp.float32), (ids & 255).astype(jnp.float32)

    ids = points_ref[pl.ds(0, sources, stride=3), :]
    mixed = points_ref[pl.ds(1, sources, stride=3), :]
    masses = points_ref[pl.ds(2, sources, stride=3), :]
    low = lax.broadcasted_iota(jnp.int32, (half, LANES), 1) < 64
    refs = (first_ref, second_ref, mass_ref)
    heads = [jnp.where(low, value[:half], pltpu.roll(value[half:], 64, 1)) for value in (ids, masses)]
    for ref, value in zip(refs, (*split(heads[0]), heads[1])):
        ref[:half, :] = value
    low = lax.broadcasted_iota(jnp.int32, (sources, LANES), 1) < 64
    live = jnp.concatenate(
        [
            jnp.max(jnp.where(low | (value == 0.0), 0.0, 1.0), axis=1, keepdims=True)
            for value in (masses, mixed)
        ],
        axis=0,
    )
    tails = packed_units(
        (
            [(value, True) for value in (*split(ids), masses)],
            [(value, False) for value in split(mixed)] + [(mixed, True)],
        ),
        live,
    )
    for i, ref in enumerate(refs):
        ref[half:, :] = tails[:, i * LANES : (i + 1) * LANES]
    rows = half + ((jnp.sum(live).astype(jnp.int32) + 1) >> 1)
    cells = acc_ref.shape[0]
    acc_ref[...] = one_hot_sum(cells, *refs, 0, ROWS)

    def more(i, carry):
        start = pl.multiple_of(ROWS + i * STEP, STEP)
        acc_ref[...] += one_hot_sum(cells, *refs, start, STEP)
        return carry

    lax.fori_loop(0, (jnp.maximum(rows - ROWS, 0) + STEP - 1) // STEP, more, 0)
    blank = jnp.zeros((STRIP, LANES), jnp.float32)
    for r in range(1, quarters):
        quarter = (here + r) & (quarters - 1)
        at = STRIP + (r - 1) * share
        before = jnp.where(quarter == 0, blank, acc_ref[at - STRIP : at, LANES:])
        after = jnp.where(quarter == quarters - 1, blank, acc_ref[at + share : at + share + STRIP, :LANES])
        rows = pl.ds(pl.multiple_of(place_of(quarter) * STRIP, STRIP), STRIP)
        store_strip(out_ref, rows, acc_ref, at, before, after)
    out_ref[pl.ds(pl.multiple_of(place_of(here) * STRIP, STRIP), STRIP), :] = jnp.zeros(
        (STRIP, out_ref.shape[1]), jnp.bfloat16
    )
    last = STRIP + (quarters - 1) * share
    side_ref[:STRIP, :] = jnp.where(here == 0, blank, acc_ref[last - STRIP : last, LANES:])
    side_ref[STRIP:, :] = jnp.where(here == quarters - 1, blank, acc_ref[STRIP : 2 * STRIP, :LANES])


def own_kernel(first_ref, second_ref, mass_ref, side_ref, out_ref, moved_ref, acc_ref):
    moved = first_ref[...] + float(out_ref.shape[1] // SPAN * STRIP - STRIP)
    moved_ref[...] = jnp.where(moved < CELLS // 2, moved, moved - CELLS)
    cells = acc_ref.shape[0]
    acc_ref[...] = one_hot_sum(cells, moved_ref, second_ref, mass_ref, 0, ROWS)
    rest = first_ref.shape[0] - ROWS

    @pl.when(jnp.max(jnp.abs(mass_ref[ROWS:, :])) > 0.0)
    def _():
        acc_ref[...] += one_hot_sum(cells, moved_ref, second_ref, mass_ref, ROWS, rest)

    before = side_ref[:STRIP, :]
    after = side_ref[STRIP:, :]
    store_strip(out_ref, pl.ds(0, STRIP), acc_ref, 0, before, after)


def band_kernel(parity_ref, kernel_ref, band_ref, odd_ref):
    parity = parity_ref[0]
    row = lax.broadcasted_iota(jnp.int32, (STRIP, 3 * TERM), 0)
    lane = lax.broadcasted_iota(jnp.int32, (STRIP, 3 * TERM), 1)
    source = lane % TERM
    near = source - PARTS
    far = near - HALO
    near = near + (1 - parity) * (STRIP + HALO)
    far = far + parity * (STRIP + HALO)
    framed = jnp.where(
        source < PARTS,
        HALO + source % STRIP,
        jnp.where(source < PARTS + HALO, near, far),
    )
    tap = framed - row
    for b in range(TAPS):
        whole = jnp.zeros(tap.shape, jnp.float32)
        for a in range(TAPS):
            whole = jnp.where(tap == a, kernel_ref[a, b], whole)
        high = whole.astype(jnp.bfloat16).astype(jnp.float32)
        rest = whole - high
        middle = rest.astype(jnp.bfloat16).astype(jnp.float32)
        term = jnp.where(lane < TERM, high, jnp.where(lane < 2 * TERM, middle, rest - middle))
        band_ref[pl.ds(b * STRIP, STRIP), :] = term
    odd_ref[...] = jnp.broadcast_to(parity.astype(jnp.float32), odd_ref.shape)


def edge_kernel(odd_ref, parts_ref, own_ref, edge_ref, *, top_if_odd):
    is_top = (odd_ref[:HALO, :] > 0.5) == top_if_odd
    for t in range(parts_ref.shape[1] // LANES):
        here = slice(t * LANES, (t + 1) * LANES)
        total = own_ref[:, here].astype(jnp.float32)
        for g in range(parts_ref.shape[0] // STRIP):
            total = total + parts_ref[g * STRIP : (g + 1) * STRIP, here].astype(jnp.float32)
        edge_ref[:, here] = jnp.where(is_top, total[:HALO], total[HALO:]).astype(jnp.bfloat16)


def smooth_kernel(band_ref, parts_ref, own_ref, near_ref, far_ref, out_ref):
    width = parts_ref.shape[1]
    near = near_ref[...].astype(jnp.float32)
    far = far_ref[...].astype(jnp.float32)
    rest = jnp.concatenate([own_ref[...].astype(jnp.float32), near, far], axis=0)
    frame = jnp.concatenate([parts_ref[...], rest.astype(jnp.bfloat16)], axis=0)
    frame = jnp.concatenate([frame, frame, frame], axis=0)
    shifted = jnp.dot(band_ref[...].astype(jnp.bfloat16), frame, preferred_element_type=jnp.float32)
    total = shifted[HALO * STRIP : (HALO + 1) * STRIP]
    for b in range(TAPS):
        if b != HALO:
            part = shifted[b * STRIP : (b + 1) * STRIP]
            total = total + pltpu.roll(part, (HALO - b) % width, 1)
    out_ref[...] = total[:, : out_ref.shape[1]]


def per_device(tile_row, pixel_col, weight, counts, kernel):
    owners = lax.axis_size("own")
    groups = lax.axis_size("grp")
    points = tile_row.shape[2] // LANES
    quarter = W // groups
    width = quarter + LANES
    packed = pl.pallas_call(
        pack_kernel,
        out_shape=jax.ShapeDtypeStruct((3 * owners, LANES), jnp.float32),
        in_specs=[pl.BlockSpec(memory_space=pltpu.HBM)] * 4,
        out_specs=vmem_spec(),
        scratch_shapes=[
            pltpu.VMEM((points, LANES), jnp.int32),
            pltpu.VMEM((points, LANES), jnp.int32),
            pltpu.VMEM((points, 1, LANES), jnp.bfloat16),
            pltpu.VMEM((1, owners), jnp.int32),
            pltpu.VMEM((points, LANES), jnp.float32),
            pltpu.VMEM((3 * owners, LANES), jnp.float32),
            pltpu.SemaphoreType.DMA((4,)),
        ],
        compiler_params=limit(4),
        name="pack",
    )(
        *(
            pltpu.with_memory_space_constraint(value.reshape(shape), pltpu.HBM)
            for value, shape in (
                (tile_row, (points, LANES)),
                (pixel_col, (points, LANES)),
                (weight, (points, 1, LANES)),
                (counts, (1, owners)),
            )
        )
    )
    order = [z * PLANE + k for z in ring_order(owners // PLANE) for k in reversed(range(PLANE))]
    arrived = lax.all_to_all(
        packed.reshape(3 * owners, 1, LANES),
        "own",
        split_axis=0,
        concat_axis=0,
        tiled=True,
        axis_index_groups=[order],
    ).reshape(3 * owners, LANES)
    plane = jax.ShapeDtypeStruct((points, LANES), jnp.float32)
    sent, side, first, second, mass = pl.pallas_call(
        others_kernel,
        out_shape=(
            jax.ShapeDtypeStruct((groups * STRIP, width), jnp.bfloat16),
            jax.ShapeDtypeStruct((2 * STRIP, LANES), jnp.float32),
            plane,
            plane,
            plane,
        ),
        in_specs=[vmem_spec()],
        out_specs=(vmem_spec(),) * 5,
        scratch_shapes=[pltpu.VMEM((CELLS - CELLS // groups + 2 * STRIP, SPAN), jnp.float32)],
        compiler_params=limit(32),
        name="others",
    )(arrived)
    sent, kernel = lax.optimization_barrier((sent, kernel))
    parts = lax.all_to_all(
        sent, "grp", split_axis=0, concat_axis=0, tiled=True, axis_index_groups=[ring_order(groups)]
    )
    own = pl.pallas_call(
        own_kernel,
        out_shape=jax.ShapeDtypeStruct((STRIP, width), jnp.bfloat16),
        in_specs=[vmem_spec()] * 4,
        out_specs=vmem_spec(),
        scratch_shapes=[
            pltpu.VMEM((points, LANES), jnp.float32),
            pltpu.VMEM((max(CELLS // groups, 256), SPAN), jnp.float32),
        ],
        compiler_params=limit(32),
        cost_estimate=pl.CostEstimate(flops=2 * points * LANES * W * STRIP // groups, bytes_accessed=2**19, transcendentals=0),
        name="own",
    )(first, second, mass, side)
    parity = (lax.axis_index("own") & 1).reshape(1).astype(jnp.int32)
    band, odd = pl.pallas_call(
        band_kernel,
        out_shape=(
            jax.ShapeDtypeStruct((TAPS * STRIP, 3 * TERM), jnp.float32),
            jax.ShapeDtypeStruct((STRIP, LANES), jnp.float32),
        ),
        in_specs=[smem_spec(), smem_spec()],
        out_specs=(vmem_spec(),) * 2,
        compiler_params=limit(4),
        name="band",
    )(parity, kernel)
    def edge(parts, top_if_odd, name):
        return pl.pallas_call(
            functools.partial(edge_kernel, top_if_odd=top_if_odd),
            out_shape=jax.ShapeDtypeStruct((HALO, width), jnp.bfloat16),
            in_specs=[vmem_spec()] * 3,
            out_specs=vmem_spec(),
            compiler_params=limit(4),
            name=name,
        )(odd, parts, own)

    near = edge(parts, True, "near")
    near, later = lax.optimization_barrier((near, parts))
    far = edge(later, False, "far")
    on_chip = [(i, i ^ 1) for i in range(owners)]
    across = [(i, i + 1) for i in range(1, owners - 1, 2)]
    across = across + [(j, i) for i, j in across]
    far = lax.ppermute(far, "own", across)
    near = lax.ppermute(near, "own", on_chip)
    return pl.pallas_call(
        smooth_kernel,
        out_shape=jax.ShapeDtypeStruct((STRIP, quarter), jnp.float32),
        in_specs=[vmem_spec()] * 5,
        out_specs=vmem_spec(),
        compiler_params=limit(16),
        name="smooth",
    )(band, parts, own, near, far)


def solution(mesh):
    placed = (
        P("grp", "own", None),
        P("grp", "own", None),
        P("grp", "own", None),
        P("grp", "own", None),
        P(),
    )
    return jax.shard_map(
        per_device, mesh=mesh, in_specs=placed, out_specs=P("own", "grp"), check_vma=False
    )
```

```python
import functools

import jax
import jax.numpy as jnp
from jax import lax
from jax.experimental import pallas as pl
from jax.experimental.pallas import tpu as pltpu
from jax.sharding import PartitionSpec as P

W = 16384
STRIP = 8
CAP = 192
LANES = 128
HALO = 4
PLANE = 8
TAPS = 2 * HALO + 1
PARTS = 40
TERM = 48
SPAN = 256
CELLS = STRIP * W // SPAN
ROWS = 136
STEP = 8


def vmem_spec():
    return pl.BlockSpec(memory_space=pltpu.VMEM)


def limit(mebibytes):
    return pltpu.CompilerParams(vmem_limit_bytes=mebibytes * 2**20)


def ring_order(length):
    half = length // 2
    order = []
    for step in range(half):
        order += [half + step, half - 1 - step]
    return order


def pack_kernel(
    row_in, col_in, weight_in, count_in, out_ref, row_ref, col_ref, weight_ref, count_ref, wide_ref, sorted_ref, sems
):
    copies = [
        pltpu.make_async_copy(source, target, sems.at[i])
        for i, (source, target) in enumerate(
            ((weight_in, weight_ref), (count_in, count_ref), (row_in, row_ref), (col_in, col_ref))
        )
    ]
    for copy in copies:
        copy.start()
    for copy in copies:
        copy.wait()
    points = row_ref.shape[0]
    planes = out_ref.shape[0] // (3 * PLANE)
    for i in range(points):
        wide_ref[pl.ds(i, 1), :] = weight_ref[i].astype(jnp.float32)
    lane = lax.broadcasted_iota(jnp.int32, (planes, LANES), 1)
    plane = lax.broadcasted_iota(jnp.int32, (planes, LANES), 0)
    counts = jnp.broadcast_to(count_ref[...], (planes, LANES))
    low = lane < 64
    half = LANES // 2
    for y in range(PLANE // 2):
        block = plane * PLANE + 2 * y
        even = jnp.sum(jnp.where(lane == block, counts, 0), axis=1, keepdims=True)
        odd = jnp.sum(jnp.where(lane == block + 1, counts, 0), axis=1, keepdims=True)
        lives = (
            lane < even,
            jnp.where(low, lane + 128, lane - 64) < jnp.where(low, even, odd),
            lane + 64 < odd,
        )
        ids, masses = [], []
        for k in range(3):
            rows = pl.ds(3 * y + k, planes, stride=3 * PLANE // 2)
            index = (((col_ref[rows, :] >> 8) * STRIP + row_ref[rows, :]) << 8) + (col_ref[rows, :] & 255)
            ids.append(index.astype(jnp.float32))
            masses.append(jnp.where(lives[k], wide_ref[rows, :], 0.0))
        for block, rows in (
            (2 * y, (ids[0], jnp.where(low, ids[1], pltpu.roll(masses[1], half, 1)), masses[0])),
            (
                2 * y + 1,
                (
                    pltpu.roll(jnp.where(low, ids[2], ids[1]), half, 1),
                    jnp.where(low, pltpu.roll(ids[2], half, 1), masses[2]),
                    pltpu.roll(jnp.where(low, masses[2], masses[1]), half, 1),
                ),
            ),
        ):
            for r, value in enumerate(rows):
                at = 3 * (PLANE - 1 - block) + r
                sorted_ref[pl.ds(at, planes, stride=3 * PLANE), :] = value
    size = 3 * PLANE
    for place, z in enumerate(ring_order(planes)):
        out_ref[pl.ds(place * size, size), :] = sorted_ref[pl.ds(z * size, size), :]


def one_hot_sum(cells, first_ref, second_ref, mass_ref, start, rows):
    first_iota = (
        lax.broadcasted_iota(jnp.int32, (cells, LANES), 0).astype(jnp.float32) - 256.0
    ).astype(jnp.bfloat16)
    second_iota = lax.broadcasted_iota(jnp.int32, (SPAN, LANES), 0).astype(jnp.float32).astype(jnp.bfloat16)
    one = jnp.ones((), jnp.bfloat16)
    zero = jnp.zeros((), jnp.bfloat16)
    here = pl.ds(start, rows)
    first = first_ref[here, :].astype(jnp.bfloat16)
    second = second_ref[here, :].astype(jnp.bfloat16)
    mass = mass_ref[here, :].astype(jnp.bfloat16)
    left, right = [], []
    for r in range(rows):
        left.append(jnp.where(first_iota == first[r : r + 1], one, zero))
        right.append(jnp.where(second_iota == second[r : r + 1], mass[r : r + 1], zero))
    return lax.dot_general(
        jnp.concatenate(left, axis=1),
        jnp.concatenate(right, axis=1),
        (((1,), (1,)), ((), ())),
        preferred_element_type=jnp.float32,
    )


def packed_units(planes, live):
    units = live.shape[0]
    count = units // 2
    low = lax.broadcasted_iota(jnp.int32, (count, LANES), 1) < 64

    def placed(value, is_high, to_high):
        moved = value if is_high == to_high else pltpu.roll(value, 64, 1)
        return jnp.where(low, 0.0, moved) if to_high else jnp.where(low, moved, 0.0)

    sources = jnp.concatenate(
        [
            jnp.concatenate([placed(value, is_high, to_high) for value, is_high in kind], axis=1)
            for to_high in (False, True)
            for kind in planes
        ],
        axis=0,
    ).astype(jnp.bfloat16)
    row = lax.broadcasted_iota(jnp.int32, (units, units), 0)
    column = lax.broadcasted_iota(jnp.int32, (units, units), 1)
    counted = jnp.where(row < column, 1.0, jnp.where(row == column, 512.0, 0.0))
    counted = (jnp.broadcast_to(live, (units, units)) * counted).astype(jnp.bfloat16)
    place = jnp.dot(jnp.ones((8, units), jnp.bfloat16), counted, preferred_element_type=jnp.float32)
    place = jnp.broadcast_to(place[:1] - 512.0, (count, units))
    target = lax.broadcasted_iota(jnp.int32, (count, units), 0).astype(jnp.float32) * 2.0
    chosen = jnp.concatenate(
        [jnp.where(place == target, 1.0, 0.0), jnp.where(place == target + 1.0, 1.0, 0.0)], axis=1
    ).astype(jnp.bfloat16)
    return jnp.dot(chosen, sources, preferred_element_type=jnp.float32)


def store_strip(out_ref, rows, acc_ref, at, before, after):
    span = out_ref.shape[1] - LANES
    for c in range(span // SPAN):
        block = acc_ref[at + c * STRIP : at + (c + 1) * STRIP, :]
        out_ref[rows, c * SPAN : (c + 1) * SPAN] = block.astype(jnp.bfloat16)
    low = lax.broadcasted_iota(jnp.int32, (STRIP, LANES), 1) < 64
    out_ref[rows, span:] = jnp.where(low, after, before).astype(jnp.bfloat16)


def others_kernel(points_ref, out_ref, side_ref, first_ref, second_ref, mass_ref, acc_ref):
    quarters = out_ref.shape[0] // STRIP
    here = lax.axis_index("grp")
    share = CELLS // quarters
    sources = points_ref.shape[0] // 3
    half = sources // 2
    origin = (here + 1) * share - STRIP

    def place_of(quarter):
        return sum(jnp.where(quarter == q, place, 0) for place, q in enumerate(ring_order(quarters)))

    def split(ids):
        ids = ids.astype(jnp.int32)
        first = ((ids >> 8) - origin) & (CELLS - 1)
        return (first - 256).astype(jnp.float32), (ids & 255).astype(jnp.float32)

    ids = points_ref[pl.ds(0, sources, stride=3), :]
    mixed = points_ref[pl.ds(1, sources, stride=3), :]
    masses = points_ref[pl.ds(2, sources, stride=3), :]
    low = lax.broadcasted_iota(jnp.int32, (half, LANES), 1) < 64
    refs = (first_ref, second_ref, mass_ref)
    heads = [jnp.where(low, value[:half], pltpu.roll(value[half:], 64, 1)) for value in (ids, masses)]
    for ref, value in zip(refs, (*split(heads[0]), heads[1])):
        ref[:half, :] = value
    low = lax.broadcasted_iota(jnp.int32, (sources, LANES), 1) < 64
    live = jnp.concatenate(
        [
            jnp.max(jnp.where(low | (value == 0.0), 0.0, 1.0), axis=1, keepdims=True)
            for value in (masses, mixed)
        ],
        axis=0,
    )
    tails = packed_units(
        (
            [(value, True) for value in (*split(ids), masses)],
            [(value, False) for value in split(mixed)] + [(mixed, True)],
        ),
        live,
    )
    for i, ref in enumerate(refs):
        ref[half:, :] = tails[:, i * LANES : (i + 1) * LANES]
    rows = half + ((jnp.sum(live).astype(jnp.int32) + 1) >> 1)
    cells = acc_ref.shape[0]
    acc_ref[...] = one_hot_sum(cells, *refs, 0, ROWS)

    def more(i, carry):
        start = pl.multiple_of(ROWS + i * STEP, STEP)
        acc_ref[...] += one_hot_sum(cells, *refs, start, STEP)
        return carry

    lax.fori_loop(0, (jnp.maximum(rows - ROWS, 0) + STEP - 1) // STEP, more, 0)
    blank = jnp.zeros((STRIP, LANES), jnp.float32)
    for r in range(1, quarters):
        quarter = (here + r) & (quarters - 1)
        at = STRIP + (r - 1) * share
        before = jnp.where(quarter == 0, blank, acc_ref[at - STRIP : at, LANES:])
        after = jnp.where(quarter == quarters - 1, blank, acc_ref[at + share : at + share + STRIP, :LANES])
        rows = pl.ds(pl.multiple_of(place_of(quarter) * STRIP, STRIP), STRIP)
        store_strip(out_ref, rows, acc_ref, at, before, after)
    out_ref[pl.ds(pl.multiple_of(place_of(here) * STRIP, STRIP), STRIP), :] = jnp.zeros(
        (STRIP, out_ref.shape[1]), jnp.bfloat16
    )
    last = STRIP + (quarters - 1) * share
    side_ref[:STRIP, :] = jnp.where(here == 0, blank, acc_ref[last - STRIP : last, LANES:])
    side_ref[STRIP:, :] = jnp.where(here == quarters - 1, blank, acc_ref[STRIP : 2 * STRIP, :LANES])


def store_band(parity, kernel_ref, band_ref):
    row = lax.broadcasted_iota(jnp.int32, (STRIP, 3 * TERM), 0)
    lane = lax.broadcasted_iota(jnp.int32, (STRIP, 3 * TERM), 1)
    source = lane % TERM
    near = source - PARTS
    far = near - HALO
    near = near + (1 - parity) * (STRIP + HALO)
    far = far + parity * (STRIP + HALO)
    framed = jnp.where(
        source < PARTS,
        HALO + source % STRIP,
        jnp.where(source < PARTS + HALO, near, far),
    )
    tap = framed - row
    for b in range(TAPS):
        whole = jnp.zeros(tap.shape, jnp.float32)
        for a in range(TAPS):
            whole = jnp.where(tap == a, kernel_ref[a, b], whole)
        high = whole.astype(jnp.bfloat16).astype(jnp.float32)
        rest = whole - high
        middle = rest.astype(jnp.bfloat16).astype(jnp.float32)
        term = jnp.where(lane < TERM, high, jnp.where(lane < 2 * TERM, middle, rest - middle))
        band_ref[pl.ds(b * STRIP, STRIP), :] = term


def own_kernel(
    first_ref, second_ref, mass_ref, side_ref, kernel_in, out_ref, band_ref, odd_ref, moved_ref, acc_ref, kernel_ref, sem
):
    copy = pltpu.make_async_copy(kernel_in, kernel_ref, sem)
    copy.start()
    moved = first_ref[...] + float(out_ref.shape[1] // SPAN * STRIP - STRIP)
    moved_ref[...] = jnp.where(moved < CELLS // 2, moved, moved - CELLS)
    cells = acc_ref.shape[0]
    acc_ref[...] = one_hot_sum(cells, moved_ref, second_ref, mass_ref, 0, ROWS)
    rest = first_ref.shape[0] - ROWS

    @pl.when(jnp.max(jnp.abs(mass_ref[ROWS:, :])) > 0.0)
    def _():
        acc_ref[...] += one_hot_sum(cells, moved_ref, second_ref, mass_ref, ROWS, rest)

    before = side_ref[:STRIP, :]
    after = side_ref[STRIP:, :]
    store_strip(out_ref, pl.ds(0, STRIP), acc_ref, 0, before, after)
    parity = lax.axis_index("own") & 1
    odd_ref[...] = jnp.broadcast_to(parity.astype(jnp.float32), odd_ref.shape)
    copy.wait()
    store_band(parity, kernel_ref, band_ref)


def edge_kernel(odd_ref, parts_ref, own_ref, edge_ref, *, top_if_odd):
    is_top = (odd_ref[:HALO, :] > 0.5) == top_if_odd
    for t in range(parts_ref.shape[1] // LANES):
        here = slice(t * LANES, (t + 1) * LANES)
        total = own_ref[:, here].astype(jnp.float32)
        for g in range(parts_ref.shape[0] // STRIP):
            total = total + parts_ref[g * STRIP : (g + 1) * STRIP, here].astype(jnp.float32)
        edge_ref[:, here] = jnp.where(is_top, total[:HALO], total[HALO:]).astype(jnp.bfloat16)


def smooth_kernel(band_ref, parts_ref, own_ref, near_ref, far_ref, out_ref):
    width = parts_ref.shape[1]
    near = near_ref[...].astype(jnp.float32)
    far = far_ref[...].astype(jnp.float32)
    rest = jnp.concatenate([own_ref[...].astype(jnp.float32), near, far], axis=0)
    frame = jnp.concatenate([parts_ref[...], rest.astype(jnp.bfloat16)], axis=0)
    frame = jnp.concatenate([frame, frame, frame], axis=0)
    shifted = jnp.dot(band_ref[...].astype(jnp.bfloat16), frame, preferred_element_type=jnp.float32)
    total = shifted[HALO * STRIP : (HALO + 1) * STRIP]
    for b in range(TAPS):
        if b != HALO:
            part = shifted[b * STRIP : (b + 1) * STRIP]
            total = total + pltpu.roll(part, (HALO - b) % width, 1)
    out_ref[...] = total[:, : out_ref.shape[1]]


def per_device(tile_row, pixel_col, weight, counts, kernel):
    owners = lax.axis_size("own")
    groups = lax.axis_size("grp")
    points = tile_row.shape[2] // LANES
    quarter = W // groups
    width = quarter + LANES
    packed = pl.pallas_call(
        pack_kernel,
        out_shape=jax.ShapeDtypeStruct((3 * owners, LANES), jnp.float32),
        in_specs=[pl.BlockSpec(memory_space=pltpu.HBM)] * 4,
        out_specs=vmem_spec(),
        scratch_shapes=[
            pltpu.VMEM((points, LANES), jnp.int32),
            pltpu.VMEM((points, LANES), jnp.int32),
            pltpu.VMEM((points, 1, LANES), jnp.bfloat16),
            pltpu.VMEM((1, owners), jnp.int32),
            pltpu.VMEM((points, LANES), jnp.float32),
            pltpu.VMEM((3 * owners, LANES), jnp.float32),
            pltpu.SemaphoreType.DMA((4,)),
        ],
        compiler_params=limit(4),
        name="pack",
    )(
        *(
            pltpu.with_memory_space_constraint(value.reshape(shape), pltpu.HBM)
            for value, shape in (
                (tile_row, (points, LANES)),
                (pixel_col, (points, LANES)),
                (weight, (points, 1, LANES)),
                (counts, (1, owners)),
            )
        )
    )
    order = [z * PLANE + k for z in ring_order(owners // PLANE) for k in reversed(range(PLANE))]
    arrived = lax.all_to_all(
        packed.reshape(3 * owners, 1, LANES),
        "own",
        split_axis=0,
        concat_axis=0,
        tiled=True,
        axis_index_groups=[order],
    ).reshape(3 * owners, LANES)
    plane = jax.ShapeDtypeStruct((points, LANES), jnp.float32)
    sent, side, first, second, mass = pl.pallas_call(
        others_kernel,
        out_shape=(
            jax.ShapeDtypeStruct((groups * STRIP, width), jnp.bfloat16),
            jax.ShapeDtypeStruct((2 * STRIP, LANES), jnp.float32),
            plane,
            plane,
            plane,
        ),
        in_specs=[vmem_spec()],
        out_specs=(vmem_spec(),) * 5,
        scratch_shapes=[pltpu.VMEM((CELLS - CELLS // groups + 2 * STRIP, SPAN), jnp.float32)],
        compiler_params=limit(32),
        name="others",
    )(arrived)
    parts = lax.all_to_all(
        sent, "grp", split_axis=0, concat_axis=0, tiled=True, axis_index_groups=[ring_order(groups)]
    )
    own, band, odd = pl.pallas_call(
        own_kernel,
        out_shape=(
            jax.ShapeDtypeStruct((STRIP, width), jnp.bfloat16),
            jax.ShapeDtypeStruct((TAPS * STRIP, 3 * TERM), jnp.float32),
            jax.ShapeDtypeStruct((STRIP, LANES), jnp.float32),
        ),
        in_specs=[vmem_spec()] * 4 + [pl.BlockSpec(memory_space=pltpu.HBM)],
        out_specs=(vmem_spec(),) * 3,
        scratch_shapes=[
            pltpu.VMEM((points, LANES), jnp.float32),
            pltpu.VMEM((max(CELLS // groups, 256), SPAN), jnp.float32),
            pltpu.SMEM(kernel.shape, jnp.float32),
            pltpu.SemaphoreType.DMA,
        ],
        compiler_params=limit(32),
        cost_estimate=pl.CostEstimate(
            flops=2 * points * LANES * W * STRIP // groups, bytes_accessed=2**19, transcendentals=0
        ),
        name="own",
    )(first, second, mass, side, pltpu.with_memory_space_constraint(kernel, pltpu.HBM))

    def edge(parts, top_if_odd, name):
        return pl.pallas_call(
            functools.partial(edge_kernel, top_if_odd=top_if_odd),
            out_shape=jax.ShapeDtypeStruct((HALO, width), jnp.bfloat16),
            in_specs=[vmem_spec()] * 3,
            out_specs=vmem_spec(),
            compiler_params=limit(4),
            name=name,
        )(odd, parts, own)

    near = edge(parts, True, "near")
    near, later = lax.optimization_barrier((near, parts))
    far = edge(later, False, "far")
    on_chip = [(i, i ^ 1) for i in range(owners)]
    across = [(i, i + 1) for i in range(1, owners - 1, 2)]
    across = across + [(j, i) for i, j in across]
    far = lax.ppermute(far, "own", across)
    near = lax.ppermute(near, "own", on_chip)
    return pl.pallas_call(
        smooth_kernel,
        out_shape=jax.ShapeDtypeStruct((STRIP, quarter), jnp.float32),
        in_specs=[vmem_spec()] * 5,
        out_specs=vmem_spec(),
        compiler_params=limit(16),
        name="smooth",
    )(band, parts, own, near, far)


def solution(mesh):
    placed = (
        P("grp", "own", None),
        P("grp", "own", None),
        P("grp", "own", None),
        P("grp", "own", None),
        P(),
    )
    return jax.shard_map(
        per_device, mesh=mesh, in_specs=placed, out_specs=P("own", "grp"), check_vma=False
    )
```

```python
import functools

import jax
import jax.numpy as jnp
from jax import lax
from jax.experimental import pallas as pl
from jax.experimental.pallas import tpu as pltpu
from jax.sharding import PartitionSpec as P

W = 16384
STRIP = 8
CAP = 192
LANES = 128
HALO = 4
PLANE = 8
PLANES = (8, 9, 7, 10, 6, 11, 5, 12, 13, 14, 2, 15, 1, 3, 4, 0)
GROUPS = (2, 3, 1, 0)
TAPS = 2 * HALO + 1
PARTS = 40
TERM = 48
SPAN = 256
CELLS = STRIP * W // SPAN
ROWS = 136
STEP = 8


def vmem_spec():
    return pl.BlockSpec(memory_space=pltpu.VMEM)


def limit(mebibytes):
    return pltpu.CompilerParams(vmem_limit_bytes=mebibytes * 2**20)


def pack_kernel(
    row_in, col_in, weight_in, count_in, out_ref, row_ref, col_ref, weight_ref, count_ref, wide_ref, sorted_ref, sems
):
    copies = [
        pltpu.make_async_copy(source, target, sems.at[i])
        for i, (source, target) in enumerate(
            ((weight_in, weight_ref), (count_in, count_ref), (row_in, row_ref), (col_in, col_ref))
        )
    ]
    for copy in copies:
        copy.start()
    for copy in copies:
        copy.wait()
    points = row_ref.shape[0]
    planes = out_ref.shape[0] // (3 * PLANE)
    for i in range(points):
        wide_ref[pl.ds(i, 1), :] = weight_ref[i].astype(jnp.float32)
    lane = lax.broadcasted_iota(jnp.int32, (planes, LANES), 1)
    plane = lax.broadcasted_iota(jnp.int32, (planes, LANES), 0)
    counts = jnp.broadcast_to(count_ref[...], (planes, LANES))
    low = lane < 64
    half = LANES // 2
    for y in range(PLANE // 2):
        block = plane * PLANE + 2 * y
        even = jnp.sum(jnp.where(lane == block, counts, 0), axis=1, keepdims=True)
        odd = jnp.sum(jnp.where(lane == block + 1, counts, 0), axis=1, keepdims=True)
        lives = (
            lane < even,
            jnp.where(low, lane + 128, lane - 64) < jnp.where(low, even, odd),
            lane + 64 < odd,
        )
        ids, masses = [], []
        for k in range(3):
            rows = pl.ds(3 * y + k, planes, stride=3 * PLANE // 2)
            index = (((col_ref[rows, :] >> 8) * STRIP + row_ref[rows, :]) << 8) + (col_ref[rows, :] & 255)
            ids.append(index.astype(jnp.float32))
            masses.append(jnp.where(lives[k], wide_ref[rows, :], 0.0))
        for block, rows in (
            (2 * y, (ids[0], jnp.where(low, ids[1], pltpu.roll(masses[1], half, 1)), masses[0])),
            (
                2 * y + 1,
                (
                    pltpu.roll(jnp.where(low, ids[2], ids[1]), half, 1),
                    jnp.where(low, pltpu.roll(ids[2], half, 1), masses[2]),
                    pltpu.roll(jnp.where(low, masses[2], masses[1]), half, 1),
                ),
            ),
        ):
            for r, value in enumerate(rows):
                at = 3 * (PLANE - 1 - block) + r
                sorted_ref[pl.ds(at, planes, stride=3 * PLANE), :] = value
    size = 3 * PLANE
    for place, z in enumerate(PLANES):
        out_ref[pl.ds(place * size, size), :] = sorted_ref[pl.ds(z * size, size), :]


def one_hot_sum(cells, first_ref, second_ref, mass_ref, start, rows):
    first_iota = (
        lax.broadcasted_iota(jnp.int32, (cells, LANES), 0).astype(jnp.float32) - 256.0
    ).astype(jnp.bfloat16)
    second_iota = lax.broadcasted_iota(jnp.int32, (SPAN, LANES), 0).astype(jnp.float32).astype(jnp.bfloat16)
    one = jnp.ones((), jnp.bfloat16)
    zero = jnp.zeros((), jnp.bfloat16)
    here = pl.ds(start, rows)
    first = first_ref[here, :].astype(jnp.bfloat16)
    second = second_ref[here, :].astype(jnp.bfloat16)
    mass = mass_ref[here, :].astype(jnp.bfloat16)
    left, right = [], []
    for r in range(rows):
        left.append(jnp.where(first_iota == first[r : r + 1], one, zero))
        right.append(jnp.where(second_iota == second[r : r + 1], mass[r : r + 1], zero))
    return lax.dot_general(
        jnp.concatenate(left, axis=1),
        jnp.concatenate(right, axis=1),
        (((1,), (1,)), ((), ())),
        preferred_element_type=jnp.float32,
    )


def packed_units(planes, live):
    units = live.shape[0]
    count = units // 2
    low = lax.broadcasted_iota(jnp.int32, (count, LANES), 1) < 64

    def placed(value, is_high, to_high):
        moved = value if is_high == to_high else pltpu.roll(value, 64, 1)
        return jnp.where(low, 0.0, moved) if to_high else jnp.where(low, moved, 0.0)

    sources = jnp.concatenate(
        [
            jnp.concatenate([placed(value, is_high, to_high) for value, is_high in kind], axis=1)
            for to_high in (False, True)
            for kind in planes
        ],
        axis=0,
    ).astype(jnp.bfloat16)
    row = lax.broadcasted_iota(jnp.int32, (units, units), 0)
    column = lax.broadcasted_iota(jnp.int32, (units, units), 1)
    counted = jnp.where(row < column, 1.0, jnp.where(row == column, 512.0, 0.0))
    counted = (jnp.broadcast_to(live, (units, units)) * counted).astype(jnp.bfloat16)
    place = jnp.dot(jnp.ones((8, units), jnp.bfloat16), counted, preferred_element_type=jnp.float32)
    place = jnp.broadcast_to(place[:1] - 512.0, (count, units))
    target = lax.broadcasted_iota(jnp.int32, (count, units), 0).astype(jnp.float32) * 2.0
    chosen = jnp.concatenate(
        [jnp.where(place == target, 1.0, 0.0), jnp.where(place == target + 1.0, 1.0, 0.0)], axis=1
    ).astype(jnp.bfloat16)
    return jnp.dot(chosen, sources, preferred_element_type=jnp.float32)


def store_strip(out_ref, rows, acc_ref, at, before, after):
    span = out_ref.shape[1] - LANES
    for c in range(span // SPAN):
        block = acc_ref[at + c * STRIP : at + (c + 1) * STRIP, :]
        out_ref[rows, c * SPAN : (c + 1) * SPAN] = block.astype(jnp.bfloat16)
    low = lax.broadcasted_iota(jnp.int32, (STRIP, LANES), 1) < 64
    out_ref[rows, span:] = jnp.where(low, after, before).astype(jnp.bfloat16)


def others_kernel(points_ref, out_ref, side_ref, first_ref, second_ref, mass_ref, acc_ref):
    quarters = out_ref.shape[0] // STRIP
    here = lax.axis_index("grp")
    share = CELLS // quarters
    sources = points_ref.shape[0] // 3
    half = sources // 2
    origin = (here + 1) * share - STRIP

    def place_of(quarter):
        return sum(jnp.where(quarter == q, place, 0) for place, q in enumerate(GROUPS))

    def split(ids):
        ids = ids.astype(jnp.int32)
        first = ((ids >> 8) - origin) & (CELLS - 1)
        return (first - 256).astype(jnp.float32), (ids & 255).astype(jnp.float32)

    ids = points_ref[pl.ds(0, sources, stride=3), :]
    mixed = points_ref[pl.ds(1, sources, stride=3), :]
    masses = points_ref[pl.ds(2, sources, stride=3), :]
    low = lax.broadcasted_iota(jnp.int32, (half, LANES), 1) < 64
    refs = (first_ref, second_ref, mass_ref)
    heads = [jnp.where(low, value[:half], pltpu.roll(value[half:], 64, 1)) for value in (ids, masses)]
    for ref, value in zip(refs, (*split(heads[0]), heads[1])):
        ref[:half, :] = value
    low = lax.broadcasted_iota(jnp.int32, (sources, LANES), 1) < 64
    live = jnp.concatenate(
        [
            jnp.max(jnp.where(low | (value == 0.0), 0.0, 1.0), axis=1, keepdims=True)
            for value in (masses, mixed)
        ],
        axis=0,
    )
    tails = packed_units(
        (
            [(value, True) for value in (*split(ids), masses)],
            [(value, False) for value in split(mixed)] + [(mixed, True)],
        ),
        live,
    )
    for i, ref in enumerate(refs):
        ref[half:, :] = tails[:, i * LANES : (i + 1) * LANES]
    rows = half + ((jnp.sum(live).astype(jnp.int32) + 1) >> 1)
    cells = acc_ref.shape[0]
    acc_ref[...] = one_hot_sum(cells, *refs, 0, ROWS)

    def more(i, carry):
        start = pl.multiple_of(ROWS + i * STEP, STEP)
        acc_ref[...] += one_hot_sum(cells, *refs, start, STEP)
        return carry

    lax.fori_loop(0, (jnp.maximum(rows - ROWS, 0) + STEP - 1) // STEP, more, 0)
    blank = jnp.zeros((STRIP, LANES), jnp.float32)
    for r in range(1, quarters):
        quarter = (here + r) & (quarters - 1)
        at = STRIP + (r - 1) * share
        before = jnp.where(quarter == 0, blank, acc_ref[at - STRIP : at, LANES:])
        after = jnp.where(quarter == quarters - 1, blank, acc_ref[at + share : at + share + STRIP, :LANES])
        rows = pl.ds(pl.multiple_of(place_of(quarter) * STRIP, STRIP), STRIP)
        store_strip(out_ref, rows, acc_ref, at, before, after)
    out_ref[pl.ds(pl.multiple_of(place_of(here) * STRIP, STRIP), STRIP), :] = jnp.zeros(
        (STRIP, out_ref.shape[1]), jnp.bfloat16
    )
    last = STRIP + (quarters - 1) * share
    side_ref[:STRIP, :] = jnp.where(here == 0, blank, acc_ref[last - STRIP : last, LANES:])
    side_ref[STRIP:, :] = jnp.where(here == quarters - 1, blank, acc_ref[STRIP : 2 * STRIP, :LANES])


def store_band(parity, kernel_ref, band_ref):
    row = lax.broadcasted_iota(jnp.int32, (STRIP, 3 * TERM), 0)
    lane = lax.broadcasted_iota(jnp.int32, (STRIP, 3 * TERM), 1)
    source = lane % TERM
    near = source - PARTS
    far = near - HALO
    near = near + (1 - parity) * (STRIP + HALO)
    far = far + parity * (STRIP + HALO)
    framed = jnp.where(
        source < PARTS,
        HALO + source % STRIP,
        jnp.where(source < PARTS + HALO, near, far),
    )
    tap = framed - row
    for b in range(TAPS):
        whole = jnp.zeros(tap.shape, jnp.float32)
        for a in range(TAPS):
            whole = jnp.where(tap == a, kernel_ref[a, b], whole)
        high = whole.astype(jnp.bfloat16).astype(jnp.float32)
        rest = whole - high
        middle = rest.astype(jnp.bfloat16).astype(jnp.float32)
        term = jnp.where(lane < TERM, high, jnp.where(lane < 2 * TERM, middle, rest - middle))
        band_ref[pl.ds(b * STRIP, STRIP), :] = term


def own_kernel(
    first_ref, second_ref, mass_ref, side_ref, kernel_in, out_ref, band_ref, odd_ref, moved_ref, acc_ref, kernel_ref, sem
):
    copy = pltpu.make_async_copy(kernel_in, kernel_ref, sem)
    copy.start()
    moved = first_ref[...] + float(out_ref.shape[1] // SPAN * STRIP - STRIP)
    moved_ref[...] = jnp.where(moved < CELLS // 2, moved, moved - CELLS)
    cells = acc_ref.shape[0]
    acc_ref[...] = one_hot_sum(cells, moved_ref, second_ref, mass_ref, 0, ROWS)
    rest = first_ref.shape[0] - ROWS

    @pl.when(jnp.max(jnp.abs(mass_ref[ROWS:, :])) > 0.0)
    def _():
        acc_ref[...] += one_hot_sum(cells, moved_ref, second_ref, mass_ref, ROWS, rest)

    before = side_ref[:STRIP, :]
    after = side_ref[STRIP:, :]
    store_strip(out_ref, pl.ds(0, STRIP), acc_ref, 0, before, after)
    parity = lax.axis_index("own") & 1
    odd_ref[...] = jnp.broadcast_to(parity.astype(jnp.float32), odd_ref.shape)
    copy.wait()
    store_band(parity, kernel_ref, band_ref)


def edge_kernel(odd_ref, parts_ref, own_ref, edge_ref, *, top_if_odd):
    is_top = (odd_ref[:HALO, :] > 0.5) == top_if_odd
    for t in range(parts_ref.shape[1] // LANES):
        here = slice(t * LANES, (t + 1) * LANES)
        total = own_ref[:, here].astype(jnp.float32)
        for g in range(parts_ref.shape[0] // STRIP):
            total = total + parts_ref[g * STRIP : (g + 1) * STRIP, here].astype(jnp.float32)
        edge_ref[:, here] = jnp.where(is_top, total[:HALO], total[HALO:]).astype(jnp.bfloat16)


def smooth_kernel(band_ref, parts_ref, own_ref, near_ref, far_ref, out_ref):
    width = parts_ref.shape[1]
    near = near_ref[...].astype(jnp.float32)
    far = far_ref[...].astype(jnp.float32)
    rest = jnp.concatenate([own_ref[...].astype(jnp.float32), near, far], axis=0)
    frame = jnp.concatenate([parts_ref[...], rest.astype(jnp.bfloat16)], axis=0)
    frame = jnp.concatenate([frame, frame, frame], axis=0)
    shifted = jnp.dot(band_ref[...].astype(jnp.bfloat16), frame, preferred_element_type=jnp.float32)
    total = shifted[HALO * STRIP : (HALO + 1) * STRIP]
    for b in range(TAPS):
        if b != HALO:
            part = shifted[b * STRIP : (b + 1) * STRIP]
            total = total + pltpu.roll(part, (HALO - b) % width, 1)
    out_ref[...] = total[:, : out_ref.shape[1]]


def per_device(tile_row, pixel_col, weight, counts, kernel):
    owners = lax.axis_size("own")
    groups = lax.axis_size("grp")
    points = tile_row.shape[2] // LANES
    quarter = W // groups
    width = quarter + LANES
    packed = pl.pallas_call(
        pack_kernel,
        out_shape=jax.ShapeDtypeStruct((3 * owners, LANES), jnp.float32),
        in_specs=[pl.BlockSpec(memory_space=pltpu.HBM)] * 4,
        out_specs=vmem_spec(),
        scratch_shapes=[
            pltpu.VMEM((points, LANES), jnp.int32),
            pltpu.VMEM((points, LANES), jnp.int32),
            pltpu.VMEM((points, 1, LANES), jnp.bfloat16),
            pltpu.VMEM((1, owners), jnp.int32),
            pltpu.VMEM((points, LANES), jnp.float32),
            pltpu.VMEM((3 * owners, LANES), jnp.float32),
            pltpu.SemaphoreType.DMA((4,)),
        ],
        compiler_params=limit(4),
        name="pack",
    )(
        *(
            pltpu.with_memory_space_constraint(value.reshape(shape), pltpu.HBM)
            for value, shape in (
                (tile_row, (points, LANES)),
                (pixel_col, (points, LANES)),
                (weight, (points, 1, LANES)),
                (counts, (1, owners)),
            )
        )
    )
    order = [z * PLANE + k for z in PLANES for k in reversed(range(PLANE))]
    arrived = lax.all_to_all(
        packed.reshape(3 * owners, 1, LANES),
        "own",
        split_axis=0,
        concat_axis=0,
        tiled=True,
        axis_index_groups=[order],
    ).reshape(3 * owners, LANES)
    plane = jax.ShapeDtypeStruct((points, LANES), jnp.float32)
    sent, side, first, second, mass = pl.pallas_call(
        others_kernel,
        out_shape=(
            jax.ShapeDtypeStruct((groups * STRIP, width), jnp.bfloat16),
            jax.ShapeDtypeStruct((2 * STRIP, LANES), jnp.float32),
            plane,
            plane,
            plane,
        ),
        in_specs=[vmem_spec()],
        out_specs=(vmem_spec(),) * 5,
        scratch_shapes=[pltpu.VMEM((CELLS - CELLS // groups + 2 * STRIP, SPAN), jnp.float32)],
        compiler_params=limit(32),
        name="others",
    )(arrived)
    parts = lax.all_to_all(
        sent, "grp", split_axis=0, concat_axis=0, tiled=True, axis_index_groups=[list(GROUPS)]
    )
    own, band, odd = pl.pallas_call(
        own_kernel,
        out_shape=(
            jax.ShapeDtypeStruct((STRIP, width), jnp.bfloat16),
            jax.ShapeDtypeStruct((TAPS * STRIP, 3 * TERM), jnp.float32),
            jax.ShapeDtypeStruct((STRIP, LANES), jnp.float32),
        ),
        in_specs=[vmem_spec()] * 4 + [pl.BlockSpec(memory_space=pltpu.HBM)],
        out_specs=(vmem_spec(),) * 3,
        scratch_shapes=[
            pltpu.VMEM((points, LANES), jnp.float32),
            pltpu.VMEM((max(CELLS // groups, 256), SPAN), jnp.float32),
            pltpu.SMEM(kernel.shape, jnp.float32),
            pltpu.SemaphoreType.DMA,
        ],
        compiler_params=limit(32),
        cost_estimate=pl.CostEstimate(
            flops=2 * points * LANES * W * STRIP // groups, bytes_accessed=2**19, transcendentals=0
        ),
        name="own",
    )(first, second, mass, side, pltpu.with_memory_space_constraint(kernel, pltpu.HBM))

    def edge(parts, top_if_odd, name):
        return pl.pallas_call(
            functools.partial(edge_kernel, top_if_odd=top_if_odd),
            out_shape=jax.ShapeDtypeStruct((HALO, width), jnp.bfloat16),
            in_specs=[vmem_spec()] * 3,
            out_specs=vmem_spec(),
            compiler_params=limit(4),
            name=name,
        )(odd, parts, own)

    near = edge(parts, True, "near")
    near, later = lax.optimization_barrier((near, parts))
    far = edge(later, False, "far")
    on_chip = [(i, i ^ 1) for i in range(owners)]
    across = [(i, i + 1) for i in range(1, owners - 1, 2)]
    across = across + [(j, i) for i, j in across]
    far = lax.ppermute(far, "own", across)
    near = lax.ppermute(near, "own", on_chip)
    return pl.pallas_call(
        smooth_kernel,
        out_shape=jax.ShapeDtypeStruct((STRIP, quarter), jnp.float32),
        in_specs=[vmem_spec()] * 5,
        out_specs=vmem_spec(),
        compiler_params=limit(16),
        name="smooth",
    )(band, parts, own, near, far)


def solution(mesh):
    placed = (
        P("grp", "own", None),
        P("grp", "own", None),
        P("grp", "own", None),
        P("grp", "own", None),
        P(),
    )
    return jax.shard_map(
        per_device, mesh=mesh, in_specs=placed, out_specs=P("own", "grp"), check_vma=False
    )
```
